32 devices in a mesh: parts: 2 (over y), frame: 4 (over z), row: 4 (over x, core).
Axes of the slice: x: 2, y: 2, z: 4, core: 2. Of those that a mesh axis runs over, the one named last changes fastest.
Arguments:
- features: bfloat16 [4, 4, 32, 32, 128], P('parts', 'frame', 'row'), parts along dimension 0, may hold values from -6 to 6
- w_in: bfloat16 [2, 3, 3, 256, 128], replicated, as said below
- b_in: float32 [2, 128], replicated, may hold values from -3 to 3
- w_mid: bfloat16 [2, 3, 3, 128, 128], replicated, may hold values from -0.1875 to 0.1875
- b_mid: float32 [2, 128], replicated, may hold values from -3 to 3
- w_out: bfloat16 [2, 3, 3, 128, 128], replicated, may hold values from -0.1875 to 0.1875
- b_out: float32 [2, 128], replicated, may hold values from -3 to 3
Outputs:
- forward_states: bfloat16 [4, 4, 32, 32, 128], P('parts', 'frame', 'row'), parts along dimension 0
- backward_states: bfloat16 [4, 4, 32, 32, 128], P('parts', 'frame', 'row'), parts along dimension 0
The draws below stay inside these ranges and needn't reach their ends.
There are 2 independent parts, one for each index of `parts`. The reference program is written for one: setup_inputs(seed, part) draws one part's arguments, and reference() takes and returns one part's arrays. A program takes and returns all parts, laid end to end along the dimension named above; an argument that names none is the same for every part. Nothing has to cross between parts.
Inputs may be any that keep to these rules, and one draw needn't show every extreme that they name: `w_in`: weights of the first convolutions.
All inputs are finite; a program needn't handle non-finite values.
Results may differ from the reference program's by a relative error of at most 0.014.
Values may be sent and summed in bfloat16 or wider, within the bound.
No kernel may reach another device: no remote copies, remote signals or barrier semaphores. Data moves between devices by JAX's collectives and lax.ppermute only.
A program may use at most 64 MiB of HBM per device.

```python
import jax
import jax.numpy as jnp
from jax import lax

CH = 128
CLIPS = 2
COLS = 32
FRAMES = 4
ROWS = 32


def draw_w_in(key, part):
    base_key = jax.random.fold_in(key, 11)
    sign_key = jax.random.fold_in(key, 23)
    spread = (18.0 * CH) ** (-0.5)
    full_shape = (2, 3, 3, 2 * CH, CH)
    base = jnp.clip(jax.random.normal(base_key, full_shape, jnp.float32), -4.0, 4.0) * spread
    signs = (jax.random.randint(sign_key, (2, CH), 0, 2) * 2 - 1).astype(jnp.float32)
    outer = signs[:, :, None] * signs[:, None, :] * (1.8 / CH)
    padded_outer = jnp.concatenate([jnp.zeros((2, CH, CH), jnp.float32), outer], axis=1)
    return base.at[:, 1, 1].add(padded_outer).astype(jnp.bfloat16)


def block_levels(rng, shape, split, least, high):
    factor_of = 1.0
    for dim, blocks in split:
        steps = jax.random.uniform(jax.random.fold_in(jax.random.fold_in(rng, 6), dim), (blocks,), jnp.float32, least / len(split), high / len(split))
        factor_of = factor_of * jnp.repeat(jnp.exp(steps), shape[dim] // blocks).reshape((-1,) + (1,) * (len(shape) - 1 - dim))
    return factor_of


def bell_draw(key, shape, deviation, reach, cuts=(), dtype=jnp.bfloat16):
    entries = jax.random.normal(key, shape, jnp.float32) * deviation
    if len(cuts) > 0:
        entries = block_levels(key, shape, cuts, -0.22, 0.18) * entries
    return jnp.clip(entries, min=-reach, max=reach).astype(dtype)


def setup_inputs(seed: int = 0, part: int = 0) -> dict:
    streams_of = jax.random.split(jax.random.key(seed), 8)
    part_splits = jax.random.split(jax.random.fold_in(streams_of[7], part), 8)
    return {
        "features": bell_draw(part_splits[0], (CLIPS, FRAMES, ROWS, COLS, CH), 1.0, 6.0, ((1, 4), (2, 4))),
        "w_in": draw_w_in(jax.random.fold_in(streams_of[7], 71), part),
        "b_in": bell_draw(streams_of[2], (2, CH), 0.5, 3.0, (), jnp.float32),
        "w_mid": bell_draw(streams_of[3], (2, 3, 3, CH, CH), (9 * CH) ** -0.5, 0.1875),
        "b_mid": bell_draw(streams_of[4], (2, CH), 0.5, 3.0, (), jnp.float32),
        "w_out": bell_draw(streams_of[5], (2, 3, 3, CH, CH), (9 * CH) ** -0.5, 0.1875),
        "b_out": bell_draw(streams_of[6], (2, CH), 0.5, 3.0, (), jnp.float32),
    }


def pad_both(field):
    return jnp.pad(field, ((1, 1), (1, 1), (0, 0)))


def conv_layer(padded, weight, bias_vec):
    row_count = padded.shape[0] - 2
    col_count = padded.shape[1] - 2
    summed = jnp.zeros((row_count, col_count, weight.shape[-1]), jnp.float32)
    for offset_y in range(3):
        for offset_x in range(3):
            window = padded[offset_y:offset_y + row_count, offset_x:offset_x + col_count, :]
            product = jnp.dot(window.reshape(row_count * col_count, window.shape[-1]), weight[offset_y, offset_x], preferred_element_type=jnp.float32)
            summed = summed + product.reshape(row_count, col_count, weight.shape[-1])
    return summed + bias_vec


def recur_step(frame_in, carried, w_in, b_in, w_mid, b_mid, w_out, b_out):
    joined = jnp.concatenate([frame_in, carried], axis=-1)
    first_act = jax.nn.gelu(conv_layer(pad_both(joined), w_in, b_in), approximate=False).astype(jnp.bfloat16)
    middle = jax.nn.gelu(conv_layer(pad_both(first_act), w_mid, b_mid), approximate=False).astype(jnp.bfloat16)
    return (first_act.astype(jnp.float32) + conv_layer(pad_both(middle), w_out, b_out)).astype(jnp.bfloat16)


def reference(features, w_in, b_in, w_mid, b_mid, w_out, b_out):
    def one_clip(frames):
        zero_state = jnp.zeros((frames.shape[1], frames.shape[2], w_out.shape[-1]), jnp.bfloat16)

        def forward_step(carried, frame_in):
            new_state = recur_step(frame_in, carried, w_in[0], b_in[0], w_mid[0], b_mid[0], w_out[0], b_out[0])
            return new_state, new_state

        def backward_step(carried, frame_in):
            new_state = recur_step(frame_in, carried, w_in[1], b_in[1], w_mid[1], b_mid[1], w_out[1], b_out[1])
            return new_state, new_state

        _, forward_seq = lax.scan(forward_step, zero_state, frames)
        _, backward_seq = lax.scan(backward_step, zero_state, frames, reverse=True)
        return forward_seq, backward_seq

    forward_states, backward_states = lax.map(one_clip, features)
    return forward_states, backward_states
```

```python
import functools

import jax
import jax.numpy as jnp
from jax import lax
from jax.experimental import pallas as pl
from jax.experimental.pallas import tpu as pltpu
from jax.sharding import PartitionSpec as P


def gelu(v):
    return 0.5 * v * (1.0 + lax.erf(v * 0.7071067811865476))


def widen(rows):
    cols = rows.shape[1]
    col = lax.broadcasted_iota(jnp.int32, rows.shape, 1)
    left = jnp.where(col == 0, 0.0, pltpu.roll(rows, 1, 1))
    right = jnp.where(col == cols - 1, 0.0, pltpu.roll(rows, cols - 1, 1))
    return jnp.concatenate([left, rows, right], axis=-1).astype(jnp.bfloat16)


class Field:
    def __init__(self, even, odd):
        self.even, self.odd = even, odd

    def clear(self):
        self.odd[0] = jnp.zeros(self.odd.shape[1:], self.odd.dtype)
        self.even[self.even.shape[0] - 1] = jnp.zeros(self.even.shape[1:], self.even.dtype)

    def zero_row(self, row):
        self.even[row // 2] = jnp.zeros(self.even.shape[1:], self.even.dtype)

    def put_row(self, row, value):
        wide = widen(value.astype(jnp.float32)[None])[0]
        if row % 2 == 0:
            self.even[row // 2] = wide
        else:
            self.odd[row // 2 + 1] = wide

    def put_pairs(self, lo, hi, first, second):
        self.even[lo:hi] = widen(first)
        self.odd[lo + 1 : hi + 1] = widen(second)

    def patches(self, lo, hi):
        n = hi - lo
        cols, wide = self.even.shape[1:]
        parts = [self.odd[lo:hi], self.even[lo:hi], self.odd[lo + 1 : hi + 1], self.even[lo + 1 : hi + 1]]
        return jnp.concatenate(parts, axis=-1).reshape(n * cols, 4 * wide)

    def centre(self, lo, hi):
        ch = self.even.shape[2] // 3
        return (
            self.even[lo:hi, :, ch : 2 * ch].astype(jnp.float32),
            self.odd[lo + 1 : hi + 1, :, ch : 2 * ch].astype(jnp.float32),
        )


def conv_pairs(field, weight, lo, hi):
    out = jnp.dot(field.patches(lo, hi), weight[...], preferred_element_type=jnp.float32)
    return out.reshape(hi - lo, field.even.shape[1], weight.shape[-1])


def split(acc, bias):
    ch = acc.shape[-1] // 2
    return acc[:, :, :ch] + bias, acc[:, :, ch:] + bias


def chunks(pairs, size):
    count = max(1, round(pairs / size))
    edges = [round(i * pairs / count) for i in range(count + 1)]
    return list(zip(edges[:-1], edges[1:]))


CHUNK = 7


def step(first_acc, sizes, first, middle, w_mid, w_out, b_in, b_mid, b_out, emit):
    n_first, n_mid, n_out = sizes
    for lo, hi in chunks(n_first, CHUNK):
        a, b = split(first_acc(lo, hi), b_in)
        first.put_pairs(lo, hi, gelu(a), gelu(b))
    for lo, hi in chunks(n_mid, CHUNK):
        a, b = split(conv_pairs(first, w_mid, lo, hi), b_mid)
        middle.put_pairs(lo, hi, gelu(a), gelu(b))
    for lo, hi in chunks(n_out, CHUNK):
        a, b = split(conv_pairs(middle, w_out, lo, hi), b_out)
        ra, rb = first.centre(lo, hi)
        emit(lo, hi, (ra + a).astype(jnp.bfloat16), (rb + b).astype(jnp.bfloat16))


def pair_sizes(rows, halo_after):
    return (rows + 3) // 2, (rows + 2) // 2, (rows + 1) // 2


def load_frame(field, rows, flip, near_ref, far_ref, height):
    depth = far_ref.shape[0]
    for i in range(rows):
        if i < height:
            value = near_ref[jnp.where(flip, height - 1 - i, i)]
        else:
            j = i - height
            value = far_ref[jnp.where(flip, depth - 1 - j, j)]
        field.put_row(i, value)


def load_either(field, rows, flip, pick, a, b, height):
    depth = a[1].shape[0]
    for i in range(rows):
        if i < height:
            at, k = jnp.where(flip, height - 1 - i, i), 0
        else:
            at, k = jnp.where(flip, depth - 1 - (i - height), i - height), 1
        field.put_row(i, jnp.where(pick, a[k][at].astype(jnp.float32), b[k][at].astype(jnp.float32)))


def pack_kernel(flags, w_in, w_mid, w_out, packed):
    flip = flags[0] == 1
    ch = w_in.shape[-1]
    zero = jnp.zeros((3 * ch, ch), packed.dtype)
    for conv in range(4):
        ref, base = [(w_in, 0), (w_in, ch), (w_mid, 0), (w_out, 0)][conv]
        for j in range(4):
            for o in range(2):
                dy = j - o
                lanes = slice(o * ch, (o + 1) * ch)
                if dy < 0 or dy > 2:
                    packed[0, conv, 3 * ch * j : 3 * ch * (j + 1), lanes] = zero
                    continue
                at = jnp.where(flip, 2 - dy, dy)
                for dx in range(3):
                    row = 3 * ch * j + ch * dx
                    packed[0, conv, row : row + ch, lanes] = ref[0, at, dx, base : base + ch, :]


def pack_weights(flags, w_in, w_mid, w_out):
    ch = w_mid.shape[-1]

    def at(p, flags):
        return (jnp.where(p == 0, flags[2], 1 - flags[2]), 0, 0, 0, 0)

    return pl.pallas_call(
        pack_kernel,
        out_shape=jax.ShapeDtypeStruct((2, 4, 12 * ch, 2 * ch), w_mid.dtype),
        grid_spec=pltpu.PrefetchScalarGridSpec(
            num_scalar_prefetch=1,
            grid=(2,),
            in_specs=[pl.BlockSpec((1,) + w.shape[1:], at) for w in (w_in, w_mid, w_out)],
            out_specs=pl.BlockSpec((1, 4, 12 * ch, 2 * ch), lambda p, flags: (p, 0, 0, 0)),
        ),
        compiler_params=pltpu.CompilerParams(vmem_limit_bytes=24 << 20),
    )(flags, w_in, w_mid, w_out)


def fields_of(refs):
    return [Field(refs[2 * i], refs[2 * i + 1]) for i in range(len(refs) // 2)]


def store_canonical(ref, flip, height, lo, hi, a, b, keep=None):
    for p in range(lo, hi):
        for o, v in ((0, a), (1, b)):
            i = 2 * p + o
            if i < height:
                at = jnp.where(flip, height - 1 - i, i)
                ref[at] = v[p - lo] if keep is None else jnp.where(keep, ref[at].astype(jnp.float32), v[p - lo].astype(jnp.float32)).astype(ref.dtype)


def first_kernel(height, flags, near_own, far_own, near_other, far_other, packed, b_in, b_mid, b_out, state, result, *scratch):
    flip, own_first = flags[0] == 1, flags[1] == 1
    bias = [b[0] for b in (b_in, b_mid, b_out)]
    w_f, w_s, w_m, w_o = (packed.at[0, i] for i in range(4))
    frame0, frame1, held, first, middle = fields_of(scratch)
    for f in (frame0, frame1, held, first, middle):
        f.clear()
    own, other = (near_own, far_own), (near_other, far_other)
    out = height + 6
    load_either(frame0, out + 6, flip, own_first, own, other, height)
    load_either(frame1, out + 3, flip, own_first, other, own, height)

    def emit_first(lo, hi, a, b):
        held.put_pairs(lo, hi, a.astype(jnp.float32), b.astype(jnp.float32))
        store_canonical(result, flip, height, lo, hi, a, b)

    n = pair_sizes(out + 3, 0)
    middle.zero_row(2 * n[2])
    step(lambda lo, hi: conv_pairs(frame0, w_f, lo, hi), n, first, middle, w_m, w_o, *bias, emit_first)

    def emit_second(lo, hi, a, b):
        for p in range(lo, hi):
            state[2 * p] = a[p - lo]
            state[2 * p + 1] = b[p - lo]
        store_canonical(result, flip, height, lo, hi, a, b, keep=own_first)

    n = pair_sizes(out, 0)
    step(
        lambda lo, hi: conv_pairs(frame1, w_f, lo, hi) + conv_pairs(held, w_s, lo, hi),
        n, first, middle, w_m, w_o, *bias, emit_second,
    )


def ahead_kernel(height, flags, near_own, far_own, near_other, far_other, packed, sums0, sums1, *scratch):
    flip, own_first = flags[0] == 1, flags[1] == 1
    frame0, frame1 = fields_of(scratch)
    for f in (frame0, frame1):
        f.clear()
    own, other = (near_own, far_own), (near_other, far_other)
    load_either(frame0, height + 7, flip, own_first, other, own, height)
    load_either(frame1, height + 3, flip, own_first, own, other, height)
    for field, sums in ((frame0, sums0), (frame1, sums1)):
        for lo, hi in chunks(sums.shape[0], CHUNK):
            sums[lo:hi] = conv_pairs(field, packed.at[0, 0], lo, hi)


def second_kernel(height, flags, incoming, sums0, sums1, packed, b_in, b_mid, b_out, result, *scratch):
    flip, own_first = flags[0] == 1, flags[1] == 1
    bias = [b[0] for b in (b_in, b_mid, b_out)]
    w_s, w_m, w_o = (packed.at[0, i] for i in range(1, 4))
    state, held, first, middle = fields_of(scratch)
    for f in (state, held, first, middle):
        f.clear()
    for i in range(height + 6):
        state.put_row(i, incoming[i])
    state.zero_row(height + 6)

    def emit_first(lo, hi, a, b):
        held.put_pairs(lo, hi, a.astype(jnp.float32), b.astype(jnp.float32))
        store_canonical(result, flip, height, lo, hi, a, b)

    n = pair_sizes(height + 3, 0)
    middle.zero_row(2 * n[2])
    step(
        lambda lo, hi: sums0[lo:hi] + conv_pairs(state, w_s, lo, hi),
        n, first, middle, w_m, w_o, *bias, emit_first,
    )

    def emit_second(lo, hi, a, b):
        keep = jnp.logical_not(own_first)
        store_canonical(result, flip, height, lo, hi, a, b, keep=keep)

    n = pair_sizes(height, 0)
    first.zero_row(2 * n[0])
    step(
        lambda lo, hi: sums1[lo:hi] + conv_pairs(held, w_s, lo, hi),
        n, first, middle, w_m, w_o, *bias, emit_second,
    )


VMEM = pl.BlockSpec(memory_space=pltpu.VMEM)
SMEM = pl.BlockSpec(memory_space=pltpu.SMEM)
LIMIT = 32 << 20


def phase_spec(shape, phase):
    return pl.BlockSpec((1,) + shape[1:], lambda i: (phase,) + (0,) * (len(shape) - 1))


def field_scratch(count, rows, cols, ch):
    return [pltpu.VMEM((rows // 2 + 1, cols, 3 * ch), jnp.bfloat16) for _ in range(2 * count)]


def paired(features, w_in, b_in, w_mid, b_mid, w_out, b_out):
    _, _, slab, cols, ch = features.shape
    height = 2 * slab
    depth = 12
    where_row, owner = lax.axis_index("row"), lax.axis_index("frame")
    core, column = where_row % 2, where_row // 2
    own_first = ((owner == 0) | (owner == 3)).astype(jnp.int32)
    late = (owner >= 2).astype(jnp.int32)
    flags = jnp.stack([column, own_first, late])
    swap_core = [(0, 1), (1, 0), (2, 3), (3, 2)]
    swap_column = [(0, 2), (2, 0), (1, 3), (3, 1)]
    swap_near = [(0, 1), (1, 0), (2, 3), (3, 2)]
    cross = [(0, 3), (3, 0), (1, 2), (2, 1)]
    swap_both = [(4 * f + r, 4 * (f ^ 1) + (r ^ 2)) for f in range(4) for r in range(4)]

    packed = pack_weights(flags, w_in, w_mid, w_out)
    biases = [jnp.stack([jnp.where(late == 1, b[1], b[0]), jnp.where(late == 1, b[0], b[1])])[:, None] for b in (b_in, b_mid, b_out)]

    mine = features[:, 0]
    kept = lax.dynamic_index_in_dim(mine, core, 0, keepdims=False)
    got = lax.ppermute(lax.dynamic_index_in_dim(mine, 1 - core, 0, keepdims=False), "row", swap_core)
    near_own = jnp.where(core == 0, jnp.concatenate([kept, got]), jnp.concatenate([got, kept]))
    edge = lax.dynamic_slice_in_dim(near_own, (height - depth) * (1 - column), depth, 0)
    near_other = lax.ppermute(near_own, "frame", swap_near)
    far_own = lax.ppermute(edge, "row", swap_column)
    far_other = lax.ppermute(edge, ("frame", "row"), swap_both)
    frames = (near_own, far_own, near_other, far_other)

    rows = height + 14
    bf16 = jnp.bfloat16
    weights_shape = packed.shape
    bias_specs = lambda phase: [phase_spec((2, 1, ch), phase)] * 3
    state, early = pl.pallas_call(
        functools.partial(first_kernel, height),
        grid=(1,),
        out_shape=(
            jax.ShapeDtypeStruct((height + 6, cols, ch), bf16),
            jax.ShapeDtypeStruct((height, cols, ch), bf16),
        ),
        in_specs=[SMEM] + [VMEM] * 4 + [phase_spec(weights_shape, 0)] + bias_specs(0),
        out_specs=(VMEM, VMEM),
        scratch_shapes=field_scratch(5, rows, cols, ch),
        compiler_params=pltpu.CompilerParams(vmem_limit_bytes=LIMIT),
    )(flags, *frames, packed, *biases)

    incoming = lax.ppermute(state, "frame", cross)
    sums = pl.pallas_call(
        functools.partial(ahead_kernel, height),
        grid=(1,),
        out_shape=tuple(jax.ShapeDtypeStruct((n, cols, 2 * ch), jnp.float32) for n in ((height + 6) // 2, (height + 3) // 2)),
        in_specs=[SMEM] + [VMEM] * 4 + [phase_spec(weights_shape, 1)],
        out_specs=(VMEM, VMEM),
        scratch_shapes=field_scratch(2, rows, cols, ch),
        compiler_params=pltpu.CompilerParams(vmem_limit_bytes=LIMIT),
    )(flags, *frames, packed)
    later = pl.pallas_call(
        functools.partial(second_kernel, height),
        grid=(1,),
        out_shape=jax.ShapeDtypeStruct((height, cols, ch), bf16),
        in_specs=[SMEM] + [VMEM] * 3 + [phase_spec(weights_shape, 1)] + bias_specs(1),
        out_specs=VMEM,
        scratch_shapes=field_scratch(4, rows, cols, ch),
        compiler_params=pltpu.CompilerParams(vmem_limit_bytes=LIMIT),
    )(flags, incoming, *sums, packed, *biases)

    both = jnp.stack([early, later])
    kept = lax.dynamic_slice_in_dim(both, slab * core, slab, 1)
    got = lax.ppermute(lax.dynamic_slice_in_dim(both, slab * (1 - core), slab, 1), "row", swap_core)
    by_clip = jnp.where(core == 0, jnp.stack([kept, got], 1), jnp.stack([got, kept], 1))
    forward = jnp.where(late == 1, by_clip[1], by_clip[0])
    backward = jnp.where(late == 1, by_clip[0], by_clip[1])
    return forward[:, None], backward[:, None]


def with_halo(block, sides, width):
    for axis, dim in sides:
        count = lax.axis_size(axis)
        forward = [(i, i + 1) for i in range(count - 1)]
        backward = [(target, source) for source, target in forward]
        low = lax.ppermute(
            lax.slice_in_dim(block, block.shape[dim] - width, None, axis=dim), axis, forward
        )
        high = lax.ppermute(lax.slice_in_dim(block, 0, width, axis=dim), axis, backward)
        block = jnp.concatenate([low, block, high], axis=dim)
    return block


def shifted(shard, axis, by):
    length = lax.axis_size(axis)
    pairs = [(i, i + by) for i in range(length) if 0 <= i + by < length]
    return lax.ppermute(shard, axis, pairs)


def conv_layer(field, weight, bias_vec):
    padded = jnp.pad(field, ((0, 0), (1, 1), (0, 0)))
    row_count = padded.shape[0] - 2
    col_count = padded.shape[1] - 2
    summed = jnp.zeros((row_count, col_count, weight.shape[-1]), jnp.float32)
    for offset_y in range(3):
        for offset_x in range(3):
            window = padded[offset_y : offset_y + row_count, offset_x : offset_x + col_count, :]
            product = jnp.dot(
                window.reshape(row_count * col_count, window.shape[-1]),
                weight[offset_y, offset_x],
                preferred_element_type=jnp.float32,
            )
            summed = summed + product.reshape(row_count, col_count, weight.shape[-1])
    return summed + bias_vec


def activate(values):
    return jax.nn.gelu(values, approximate=False)


def pipelined(features, w_in, b_in, w_mid, b_mid, w_out, b_out):
    clip_count, frame_count, row_count, col_count, channels = features.shape
    owners = lax.axis_size("frame")
    owner_pos = lax.axis_index("frame")
    section_total = owners + clip_count - 1
    rim_depth = 3
    rimmed = with_halo(features, (("row", 2),), rim_depth)
    slab_start = lax.axis_index("row") * row_count
    total_rows = row_count * lax.axis_size("row")
    outer_rows = slab_start - 2 + jnp.arange(row_count + 4, dtype=jnp.int32)
    outer_mask = ((outer_rows >= 0) & (outer_rows < total_rows)).astype(jnp.float32)[:, None, None]
    inner_rows = slab_start - 1 + jnp.arange(row_count + 2, dtype=jnp.int32)
    inner_mask = ((inner_rows >= 0) & (inner_rows < total_rows)).astype(jnp.float32)[:, None, None]
    zero_state = jnp.zeros((row_count, col_count, channels), jnp.bfloat16)

    def skipped(operand):
        return zero_state

    def frame_step(frame_rim, carried, direction, is_live):
        state_rim = with_halo(carried, (("row", 0),), rim_depth)
        joined = jnp.concatenate([frame_rim, state_rim], axis=-1)

        def compute(joined_in):
            first_act = (
                activate(conv_layer(joined_in, w_in[direction], b_in[direction])) * outer_mask
            ).astype(jnp.bfloat16)
            middle = (
                activate(conv_layer(first_act, w_mid[direction], b_mid[direction])) * inner_mask
            ).astype(jnp.bfloat16)
            residual = first_act[2:-2].astype(jnp.float32)
            return (residual + conv_layer(middle, w_out[direction], b_out[direction])).astype(
                jnp.bfloat16
            )

        return lax.cond(is_live, compute, skipped, joined)

    def sweep_section(section_num, incoming, outputs, direction):
        position = owner_pos if direction == 0 else owners - 1 - owner_pos
        clip_index = section_num - position
        is_live = (clip_index >= 0) & (clip_index < clip_count)
        chosen = jnp.clip(clip_index, 0, clip_count - 1)
        clip_frames = lax.dynamic_index_in_dim(rimmed, chosen, 0, keepdims=False)
        clip_out = lax.dynamic_index_in_dim(outputs, chosen, 0, keepdims=False)
        carried = incoming
        frame_order = range(frame_count) if direction == 0 else range(frame_count - 1, -1, -1)
        for frame_slot in frame_order:
            carried = frame_step(clip_frames[frame_slot], carried, direction, is_live)
            clip_out = clip_out.at[frame_slot].set(
                jnp.where(is_live, carried, clip_out[frame_slot])
            )
        outputs = lax.dynamic_update_index_in_dim(outputs, clip_out, chosen, 0)
        if direction == 0:
            passed = shifted(carried, "frame", 1)
        else:
            passed = shifted(carried, "frame", -1)
        return (passed, outputs)

    blank_out = jnp.zeros_like(features)

    def forward_turn(section_num, carry):
        return sweep_section(section_num, carry[0], carry[1], 0)

    def backward_turn(section_num, carry):
        return sweep_section(section_num, carry[0], carry[1], 1)

    _, forward_states = lax.fori_loop(0, section_total, forward_turn, (zero_state, blank_out))
    _, backward_states = lax.fori_loop(0, section_total, backward_turn, (zero_state, blank_out))
    return (forward_states, backward_states)


def on_device(features, *weights):
    clips, frames, slab, _, _ = features.shape
    fits = (clips, frames, lax.axis_size("frame"), lax.axis_size("row")) == (2, 1, 4, 4) and slab >= 6
    return (paired if fits else pipelined)(features, *weights)


def solution(mesh):
    placed = (P("parts", "frame", "row", None, None), P(), P(), P(), P(), P(), P())
    return jax.shard_map(
        on_device,
        mesh=mesh,
        in_specs=placed,
        out_specs=(P("parts", "frame", "row", None, None), P("parts", "frame", "row", None, None)),
        check_vma=False,
    )
```

```python
import functools

import jax
import jax.numpy as jnp
from jax import lax
from jax.experimental import pallas as pl
from jax.experimental.pallas import tpu as pltpu
from jax.sharding import PartitionSpec as P


def gelu(v):
    return 0.5 * v * (1.0 + lax.erf(v * 0.7071067811865476))


def widen(rows):
    cols = rows.shape[1]
    col = lax.broadcasted_iota(jnp.int32, rows.shape, 1)
    left = jnp.where(col == 0, 0.0, pltpu.roll(rows, 1, 1))
    right = jnp.where(col == cols - 1, 0.0, pltpu.roll(rows, cols - 1, 1))
    return jnp.concatenate([left, rows, right], axis=-1).astype(jnp.bfloat16)


class Field:
    def __init__(self, even, odd):
        self.even, self.odd = even, odd

    def clear(self):
        self.odd[0] = jnp.zeros(self.odd.shape[1:], self.odd.dtype)
        self.even[self.even.shape[0] - 1] = jnp.zeros(self.even.shape[1:], self.even.dtype)

    def zero_row(self, row):
        self.even[row // 2] = jnp.zeros(self.even.shape[1:], self.even.dtype)

    def put_row(self, row, value):
        wide = widen(value.astype(jnp.float32)[None])[0]
        if row % 2 == 0:
            self.even[row // 2] = wide
        else:
            self.odd[row // 2 + 1] = wide

    def put_pairs(self, lo, hi, first, second):
        self.even[lo:hi] = widen(first)
        self.odd[lo + 1 : hi + 1] = widen(second)

    def patches(self, lo, hi):
        n = hi - lo
        cols, wide = self.even.shape[1:]
        parts = [self.odd[lo:hi], self.even[lo:hi], self.odd[lo + 1 : hi + 1], self.even[lo + 1 : hi + 1]]
        return jnp.concatenate(parts, axis=-1).reshape(n * cols, 4 * wide)

    def centre(self, lo, hi):
        ch = self.even.shape[2] // 3
        return (
            self.even[lo:hi, :, ch : 2 * ch].astype(jnp.float32),
            self.odd[lo + 1 : hi + 1, :, ch : 2 * ch].astype(jnp.float32),
        )


def conv_pairs(field, weight, lo, hi):
    out = jnp.dot(field.patches(lo, hi), weight[...], preferred_element_type=jnp.float32)
    return out.reshape(hi - lo, field.even.shape[1], weight.shape[-1])


def split(acc, bias):
    ch = acc.shape[-1] // 2
    return acc[:, :, :ch] + bias, acc[:, :, ch:] + bias


def chunks(pairs, size):
    count = max(1, round(pairs / size))
    edges = [round(i * pairs / count) for i in range(count + 1)]
    return list(zip(edges[:-1], edges[1:]))


CHUNK = 7


def step(first_acc, sizes, first, middle, w_mid, w_out, b_in, b_mid, b_out, emit):
    n_first, n_mid, n_out = sizes
    for lo, hi in chunks(n_first, CHUNK):
        a, b = split(first_acc(lo, hi), b_in)
        first.put_pairs(lo, hi, gelu(a), gelu(b))
    for lo, hi in chunks(n_mid, CHUNK):
        a, b = split(conv_pairs(first, w_mid, lo, hi), b_mid)
        middle.put_pairs(lo, hi, gelu(a), gelu(b))
    for lo, hi in chunks(n_out, CHUNK):
        a, b = split(conv_pairs(middle, w_out, lo, hi), b_out)
        ra, rb = first.centre(lo, hi)
        emit(lo, hi, (ra + a).astype(jnp.bfloat16), (rb + b).astype(jnp.bfloat16))


def pair_sizes(rows, halo_after):
    return (rows + 3) // 2, (rows + 2) // 2, (rows + 1) // 2


def load_frame(field, rows, flip, near_ref, far_ref, height):
    depth = far_ref.shape[0]
    for i in range(rows):
        if i < height:
            value = near_ref[jnp.where(flip, height - 1 - i, i)]
        else:
            j = i - height
            value = far_ref[jnp.where(flip, depth - 1 - j, j)]
        field.put_row(i, value)


def load_either(field, rows, flip, pick, a, b, height):
    depth = a[1].shape[0]
    for i in range(rows):
        if i < height:
            at, k = jnp.where(flip, height - 1 - i, i), 0
        else:
            at, k = jnp.where(flip, depth - 1 - (i - height), i - height), 1
        field.put_row(i, jnp.where(pick, a[k][at].astype(jnp.float32), b[k][at].astype(jnp.float32)))


def pack_kernel(phase, flags, w_in, w_mid, w_out, packed):
    flip = flags[0] == 1
    ch = w_in.shape[-1]
    zero = jnp.zeros((3 * ch, ch), packed.dtype)
    for conv in range(4):
        ref, base = [(w_in, 0), (w_in, ch), (w_mid, 0), (w_out, 0)][conv]
        for j in range(4):
            for o in range(2):
                dy = j - o
                lanes = slice(o * ch, (o + 1) * ch)
                if dy < 0 or dy > 2:
                    packed[conv, 3 * ch * j : 3 * ch * (j + 1), lanes] = zero
                    continue
                at = jnp.where(flip, 2 - dy, dy)
                for dx in range(3):
                    row = 3 * ch * j + ch * dx
                    packed[conv, row : row + ch, lanes] = ref[0, at, dx, base : base + ch, :]


def pack_weights(phase, flags, w_in, w_mid, w_out):
    ch = w_mid.shape[-1]

    def at(i, flags):
        return (flags[2] if phase == 0 else 1 - flags[2], 0, 0, 0, 0)

    return pl.pallas_call(
        functools.partial(pack_kernel, phase),
        out_shape=jax.ShapeDtypeStruct((4, 12 * ch, 2 * ch), w_mid.dtype),
        grid_spec=pltpu.PrefetchScalarGridSpec(
            num_scalar_prefetch=1,
            grid=(1,),
            in_specs=[pl.BlockSpec((1,) + w.shape[1:], at) for w in (w_in, w_mid, w_out)],
            out_specs=pl.BlockSpec(memory_space=pltpu.VMEM),
        ),
        cost_estimate=pl.CostEstimate(flops=0, bytes_accessed=8 << 20, transcendentals=0),
        compiler_params=pltpu.CompilerParams(vmem_limit_bytes=12 << 20),
    )(flags, w_in, w_mid, w_out)


def fields_of(refs):
    return [Field(refs[2 * i], refs[2 * i + 1]) for i in range(len(refs) // 2)]


def biases_of(direction, *refs):
    return [jnp.where(direction == 1, ref[1], ref[0]) for ref in refs]


def store_canonical(ref, flip, height, lo, hi, a, b, keep=None):
    for p in range(lo, hi):
        for o, v in ((0, a), (1, b)):
            i = 2 * p + o
            if i < height:
                at = jnp.where(flip, height - 1 - i, i)
                ref[at] = v[p - lo] if keep is None else jnp.where(keep, ref[at].astype(jnp.float32), v[p - lo].astype(jnp.float32)).astype(ref.dtype)


def first_kernel(height, flags, near_own, far_own, near_other, far_other, packed, b_in, b_mid, b_out, state, result, *scratch):
    flip, own_first = flags[0] == 1, flags[1] == 1
    bias = biases_of(flags[2], b_in, b_mid, b_out)
    w_f, w_s, w_m, w_o = (packed.at[i] for i in range(4))
    frame0, frame1, held, first, middle = fields_of(scratch)
    for f in (frame0, frame1, held, first, middle):
        f.clear()
    own, other = (near_own, far_own), (near_other, far_other)
    out = height + 6
    load_either(frame0, out + 6, flip, own_first, own, other, height)
    load_either(frame1, out + 3, flip, own_first, other, own, height)

    def emit_first(lo, hi, a, b):
        held.put_pairs(lo, hi, a.astype(jnp.float32), b.astype(jnp.float32))
        store_canonical(result, flip, height, lo, hi, a, b)

    n = pair_sizes(out + 3, 0)
    middle.zero_row(2 * n[2])
    step(lambda lo, hi: conv_pairs(frame0, w_f, lo, hi), n, first, middle, w_m, w_o, *bias, emit_first)

    def emit_second(lo, hi, a, b):
        for p in range(lo, hi):
            state[2 * p] = a[p - lo]
            state[2 * p + 1] = b[p - lo]
        store_canonical(result, flip, height, lo, hi, a, b, keep=own_first)

    n = pair_sizes(out, 0)
    step(
        lambda lo, hi: conv_pairs(frame1, w_f, lo, hi) + conv_pairs(held, w_s, lo, hi),
        n, first, middle, w_m, w_o, *bias, emit_second,
    )


def ahead_kernel(height, flags, near_own, far_own, near_other, far_other, packed, sums0, sums1, *scratch):
    flip, own_first = flags[0] == 1, flags[1] == 1
    frame0, frame1 = fields_of(scratch)
    for f in (frame0, frame1):
        f.clear()
    own, other = (near_own, far_own), (near_other, far_other)
    load_either(frame0, height + 7, flip, own_first, other, own, height)
    load_either(frame1, height + 3, flip, own_first, own, other, height)
    for field, sums in ((frame0, sums0), (frame1, sums1)):
        for lo, hi in chunks(sums.shape[0], CHUNK):
            sums[lo:hi] = conv_pairs(field, packed.at[0], lo, hi)


def second_kernel(height, flags, incoming, sums0, sums1, packed, b_in, b_mid, b_out, result, *scratch):
    flip, own_first = flags[0] == 1, flags[1] == 1
    bias = biases_of(1 - flags[2], b_in, b_mid, b_out)
    w_s, w_m, w_o = (packed.at[i] for i in range(1, 4))
    state, held, first, middle = fields_of(scratch)
    for f in (state, held, first, middle):
        f.clear()
    for i in range(height + 6):
        state.put_row(i, incoming[i])
    state.zero_row(height + 6)

    def emit_first(lo, hi, a, b):
        held.put_pairs(lo, hi, a.astype(jnp.float32), b.astype(jnp.float32))
        store_canonical(result, flip, height, lo, hi, a, b)

    n = pair_sizes(height + 3, 0)
    middle.zero_row(2 * n[2])
    step(
        lambda lo, hi: sums0[lo:hi] + conv_pairs(state, w_s, lo, hi),
        n, first, middle, w_m, w_o, *bias, emit_first,
    )

    def emit_second(lo, hi, a, b):
        keep = jnp.logical_not(own_first)
        store_canonical(result, flip, height, lo, hi, a, b, keep=keep)

    n = pair_sizes(height, 0)
    first.zero_row(2 * n[0])
    step(
        lambda lo, hi: sums1[lo:hi] + conv_pairs(held, w_s, lo, hi),
        n, first, middle, w_m, w_o, *bias, emit_second,
    )


VMEM = pl.BlockSpec(memory_space=pltpu.VMEM)
SMEM = pl.BlockSpec(memory_space=pltpu.SMEM)
LIMIT = 24 << 20


def field_scratch(count, rows, cols, ch):
    return [pltpu.VMEM((rows // 2 + 1, cols, 3 * ch), jnp.bfloat16) for _ in range(2 * count)]


def paired(features, w_in, b_in, w_mid, b_mid, w_out, b_out):
    _, _, slab, cols, ch = features.shape
    height = 2 * slab
    depth = 12
    where_row, owner = lax.axis_index("row"), lax.axis_index("frame")
    core, column = where_row % 2, where_row // 2
    own_first = ((owner == 0) | (owner == 3)).astype(jnp.int32)
    late = (owner >= 2).astype(jnp.int32)
    flags = jnp.stack([column, own_first, late])
    swap_core = [(0, 1), (1, 0), (2, 3), (3, 2)]
    swap_column = [(0, 2), (2, 0), (1, 3), (3, 1)]
    swap_near = [(0, 1), (1, 0), (2, 3), (3, 2)]
    cross = [(0, 3), (3, 0), (1, 2), (2, 1)]
    swap_both = [(4 * f + r, 4 * (f ^ 1) + (r ^ 2)) for f in range(4) for r in range(4)]

    biases = (b_in, b_mid, b_out)
    mine = features[:, 0]
    kept = lax.dynamic_index_in_dim(mine, core, 0, keepdims=False)
    got = lax.ppermute(lax.dynamic_index_in_dim(mine, 1 - core, 0, keepdims=False), "row", swap_core)
    near_own = jnp.where(core == 0, jnp.concatenate([kept, got]), jnp.concatenate([got, kept]))
    edge = lax.dynamic_slice_in_dim(near_own, (height - depth) * (1 - column), depth, 0)
    near_other = lax.ppermute(near_own, "frame", swap_near)
    far_own = lax.ppermute(edge, "row", swap_column)
    far_other = lax.ppermute(edge, ("frame", "row"), swap_both)
    frames = (near_own, far_own, near_other, far_other)

    rows = height + 14
    bf16 = jnp.bfloat16
    cost = lambda rows: pl.CostEstimate(flops=rows * cols * ch * ch * 24, bytes_accessed=4 << 20, transcendentals=0)
    held_flags, _ = lax.optimization_barrier((flags, near_own))
    packed = pack_weights(0, held_flags, w_in, w_mid, w_out)
    state, early = pl.pallas_call(
        functools.partial(first_kernel, height),
        grid=(1,),
        out_shape=(
            jax.ShapeDtypeStruct((height + 6, cols, ch), bf16),
            jax.ShapeDtypeStruct((height, cols, ch), bf16),
        ),
        in_specs=[SMEM] + [VMEM] * 8,
        out_specs=(VMEM, VMEM),
        scratch_shapes=field_scratch(5, rows, cols, ch),
        cost_estimate=cost(250),
        compiler_params=pltpu.CompilerParams(vmem_limit_bytes=LIMIT),
    )(flags, *frames, packed, *biases)

    held_flags, _ = lax.optimization_barrier((flags, state))
    packed = pack_weights(1, held_flags, w_in, w_mid, w_out)
    incoming = lax.ppermute(state, "frame", cross)
    sums = pl.pallas_call(
        functools.partial(ahead_kernel, height),
        grid=(1,),
        out_shape=tuple(jax.ShapeDtypeStruct((n, cols, 2 * ch), jnp.float32) for n in ((height + 6) // 2, (height + 3) // 2)),
        in_specs=[SMEM] + [VMEM] * 5,
        out_specs=(VMEM, VMEM),
        scratch_shapes=field_scratch(2, rows, cols, ch),
        cost_estimate=cost(42),
        compiler_params=pltpu.CompilerParams(vmem_limit_bytes=LIMIT),
    )(flags, *frames, packed)
    later = pl.pallas_call(
        functools.partial(second_kernel, height),
        grid=(1,),
        out_shape=jax.ShapeDtypeStruct((height, cols, ch), bf16),
        in_specs=[SMEM] + [VMEM] * 7,
        out_specs=VMEM,
        scratch_shapes=field_scratch(4, rows, cols, ch),
        cost_estimate=cost(120),
        compiler_params=pltpu.CompilerParams(vmem_limit_bytes=LIMIT),
    )(flags, incoming, *sums, packed, *biases)

    both = jnp.stack([early, later])
    kept = lax.dynamic_slice_in_dim(both, slab * core, slab, 1)
    got = lax.ppermute(lax.dynamic_slice_in_dim(both, slab * (1 - core), slab, 1), "row", swap_core)
    by_clip = jnp.where(core == 0, jnp.stack([kept, got], 1), jnp.stack([got, kept], 1))
    forward = jnp.where(late == 1, by_clip[1], by_clip[0])
    backward = jnp.where(late == 1, by_clip[0], by_clip[1])
    return forward[:, None], backward[:, None]


def with_halo(block, sides, width):
    for axis, dim in sides:
        count = lax.axis_size(axis)
        forward = [(i, i + 1) for i in range(count - 1)]
        backward = [(target, source) for source, target in forward]
        low = lax.ppermute(
            lax.slice_in_dim(block, block.shape[dim] - width, None, axis=dim), axis, forward
        )
        high = lax.ppermute(lax.slice_in_dim(block, 0, width, axis=dim), axis, backward)
        block = jnp.concatenate([low, block, high], axis=dim)
    return block


def shifted(shard, axis, by):
    length = lax.axis_size(axis)
    pairs = [(i, i + by) for i in range(length) if 0 <= i + by < length]
    return lax.ppermute(shard, axis, pairs)


def conv_layer(field, weight, bias_vec):
    padded = jnp.pad(field, ((0, 0), (1, 1), (0, 0)))
    row_count = padded.shape[0] - 2
    col_count = padded.shape[1] - 2
    summed = jnp.zeros((row_count, col_count, weight.shape[-1]), jnp.float32)
    for offset_y in range(3):
        for offset_x in range(3):
            window = padded[offset_y : offset_y + row_count, offset_x : offset_x + col_count, :]
            product = jnp.dot(
                window.reshape(row_count * col_count, window.shape[-1]),
                weight[offset_y, offset_x],
                preferred_element_type=jnp.float32,
            )
            summed = summed + product.reshape(row_count, col_count, weight.shape[-1])
    return summed + bias_vec


def activate(values):
    return jax.nn.gelu(values, approximate=False)


def pipelined(features, w_in, b_in, w_mid, b_mid, w_out, b_out):
    clip_count, frame_count, row_count, col_count, channels = features.shape
    owners = lax.axis_size("frame")
    owner_pos = lax.axis_index("frame")
    section_total = owners + clip_count - 1
    rim_depth = 3
    rimmed = with_halo(features, (("row", 2),), rim_depth)
    slab_start = lax.axis_index("row") * row_count
    total_rows = row_count * lax.axis_size("row")
    outer_rows = slab_start - 2 + jnp.arange(row_count + 4, dtype=jnp.int32)
    outer_mask = ((outer_rows >= 0) & (outer_rows < total_rows)).astype(jnp.float32)[:, None, None]
    inner_rows = slab_start - 1 + jnp.arange(row_count + 2, dtype=jnp.int32)
    inner_mask = ((inner_rows >= 0) & (inner_rows < total_rows)).astype(jnp.float32)[:, None, None]
    zero_state = jnp.zeros((row_count, col_count, channels), jnp.bfloat16)

    def skipped(operand):
        return zero_state

    def frame_step(frame_rim, carried, direction, is_live):
        state_rim = with_halo(carried, (("row", 0),), rim_depth)
        joined = jnp.concatenate([frame_rim, state_rim], axis=-1)

        def compute(joined_in):
            first_act = (
                activate(conv_layer(joined_in, w_in[direction], b_in[direction])) * outer_mask
            ).astype(jnp.bfloat16)
            middle = (
                activate(conv_layer(first_act, w_mid[direction], b_mid[direction])) * inner_mask
            ).astype(jnp.bfloat16)
            residual = first_act[2:-2].astype(jnp.float32)
            return (residual + conv_layer(middle, w_out[direction], b_out[direction])).astype(
                jnp.bfloat16
            )

        return lax.cond(is_live, compute, skipped, joined)

    def sweep_section(section_num, incoming, outputs, direction):
        position = owner_pos if direction == 0 else owners - 1 - owner_pos
        clip_index = section_num - position
        is_live = (clip_index >= 0) & (clip_index < clip_count)
        chosen = jnp.clip(clip_index, 0, clip_count - 1)
        clip_frames = lax.dynamic_index_in_dim(rimmed, chosen, 0, keepdims=False)
        clip_out = lax.dynamic_index_in_dim(outputs, chosen, 0, keepdims=False)
        carried = incoming
        frame_order = range(frame_count) if direction == 0 else range(frame_count - 1, -1, -1)
        for frame_slot in frame_order:
            carried = frame_step(clip_frames[frame_slot], carried, direction, is_live)
            clip_out = clip_out.at[frame_slot].set(
                jnp.where(is_live, carried, clip_out[frame_slot])
            )
        outputs = lax.dynamic_update_index_in_dim(outputs, clip_out, chosen, 0)
        if direction == 0:
            passed = shifted(carried, "frame", 1)
        else:
            passed = shifted(carried, "frame", -1)
        return (passed, outputs)

    blank_out = jnp.zeros_like(features)

    def forward_turn(section_num, carry):
        return sweep_section(section_num, carry[0], carry[1], 0)

    def backward_turn(section_num, carry):
        return sweep_section(section_num, carry[0], carry[1], 1)

    _, forward_states = lax.fori_loop(0, section_total, forward_turn, (zero_state, blank_out))
    _, backward_states = lax.fori_loop(0, section_total, backward_turn, (zero_state, blank_out))
    return (forward_states, backward_states)


def on_device(features, *weights):
    clips, frames, slab, _, _ = features.shape
    fits = (clips, frames, lax.axis_size("frame"), lax.axis_size("row")) == (2, 1, 4, 4) and slab >= 6
    return (paired if fits else pipelined)(features, *weights)


def solution(mesh):
    placed = (P("parts", "frame", "row", None, None), P(), P(), P(), P(), P(), P())
    return jax.shard_map(
        on_device,
        mesh=mesh,
        in_specs=placed,
        out_specs=(P("parts", "frame", "row", None, None), P("parts", "frame", "row", None, None)),
        check_vma=False,
    )
```

```python
import functools

import jax
import jax.numpy as jnp
from jax import lax
from jax.experimental import pallas as pl
from jax.experimental.pallas import tpu as pltpu
from jax.sharding import PartitionSpec as P


def gelu(v):
    return 0.5 * v * (1.0 + lax.erf(v * 0.7071067811865476))


def widen(rows):
    cols = rows.shape[1]
    col = lax.broadcasted_iota(jnp.int32, rows.shape, 1)
    left = jnp.where(col == 0, 0.0, pltpu.roll(rows, 1, 1))
    right = jnp.where(col == cols - 1, 0.0, pltpu.roll(rows, cols - 1, 1))
    return jnp.concatenate([left, rows, right], axis=-1).astype(jnp.bfloat16)


class Field:
    def __init__(self, even, odd):
        self.even, self.odd = even, odd

    def clear(self):
        self.odd[0] = jnp.zeros(self.odd.shape[1:], self.odd.dtype)

    def zero_row(self, row):
        self.even[row // 2] = jnp.zeros(self.even.shape[1:], self.even.dtype)

    def put_row(self, row, value):
        wide = widen(value.astype(jnp.float32)[None])[0]
        if row % 2 == 0:
            self.even[row // 2] = wide
        else:
            self.odd[row // 2 + 1] = wide

    def put_pairs(self, lo, hi, first, second):
        self.even[lo:hi] = widen(first)
        self.odd[lo + 1 : hi + 1] = widen(second)

    def patches(self, lo, hi):
        n = hi - lo
        cols, wide = self.even.shape[1:]
        parts = [self.odd[lo:hi], self.even[lo:hi], self.odd[lo + 1 : hi + 1], self.even[lo + 1 : hi + 1]]
        return jnp.concatenate(parts, axis=-1).reshape(n * cols, 4 * wide)

    def centre(self, lo, hi):
        ch = self.even.shape[2] // 3
        return (
            self.even[lo:hi, :, ch : 2 * ch].astype(jnp.float32),
            self.odd[lo + 1 : hi + 1, :, ch : 2 * ch].astype(jnp.float32),
        )


def conv_pairs(field, weight, lo, hi):
    out = jnp.dot(field.patches(lo, hi), weight[...], preferred_element_type=jnp.float32)
    return out.reshape(hi - lo, field.even.shape[1], weight.shape[-1])


def split(acc, bias):
    ch = acc.shape[-1] // 2
    return acc[:, :, :ch] + bias, acc[:, :, ch:] + bias


SPLIT = 7


def run(stages):
    waiting = []

    def finish_to(count):
        while len(waiting) > count:
            done = waiting.pop(0)
            done[0](*done[1:])

    for s, (pairs, sums, finish) in enumerate(stages):
        edge = min(max(SPLIT - s, 0), pairs)
        if edge == 0 or edge == pairs:
            finish_to(0)
            waiting.append((finish, 0, pairs, sums(0, pairs)))
            continue
        finish_to(1)
        waiting.append((finish, 0, edge, sums(0, edge)))
        finish_to(1)
        waiting.append((finish, edge, pairs, sums(edge, pairs)))
    finish_to(0)


def frame_stages(first_sums, sizes, first, middle, w_mid, w_out, b_in, b_mid, b_out, emit):
    def activated(field, bias):
        def finish(lo, hi, acc):
            a, b = split(acc, bias)
            field.put_pairs(lo, hi, gelu(a), gelu(b))

        return finish

    def add(lo, hi, acc):
        a, b = split(acc, b_out)
        ra, rb = first.centre(lo, hi)
        emit(lo, hi, (ra + a).astype(jnp.bfloat16), (rb + b).astype(jnp.bfloat16))

    return [
        (sizes[0], first_sums, activated(first, b_in)),
        (sizes[1], lambda lo, hi: conv_pairs(first, w_mid, lo, hi), activated(middle, b_mid)),
        (sizes[2], lambda lo, hi: conv_pairs(middle, w_out, lo, hi), add),
    ]


def pair_sizes(rows):
    return (rows + 3) // 2, (rows + 2) // 2, (rows + 1) // 2


def load_either(field, rows, flip, pick, a, b, height):
    depth = a[1].shape[0]
    for i in range(rows):
        if i < height:
            at, k = jnp.where(flip, height - 1 - i, i), 0
        else:
            at, k = jnp.where(flip, depth - 1 - (i - height), i - height), 1
        field.put_row(i, jnp.where(pick, a[k][at].astype(jnp.float32), b[k][at].astype(jnp.float32)))


def pack_kernel(phase, parts, flags, *refs):
    flip = flags[0] == 1
    direction = flags[2] if phase == 0 else 1 - flags[2]
    packed = refs[-1]
    ch = packed.shape[-1] // 2
    zero = jnp.zeros((3 * ch, ch), packed.dtype)
    for conv, (which, base) in enumerate(parts):
        packed[conv, 9 * ch : 12 * ch, :ch] = zero
        packed[conv, : 3 * ch, ch:] = zero
        for dy in range(3):
            at = jnp.where(flip, 2 - dy, dy)
            for dx in range(3):
                taps = refs[which][direction, at, dx, base : base + ch, :]
                for o in range(2):
                    row = 3 * ch * (dy + o) + ch * dx
                    packed[conv, row : row + ch, o * ch : (o + 1) * ch] = taps


def pack_weights(phase, parts, flags, *weights):
    ch = weights[0].shape[-1]
    return pl.pallas_call(
        functools.partial(pack_kernel, phase, parts),
        out_shape=jax.ShapeDtypeStruct((len(parts), 12 * ch, 2 * ch), weights[0].dtype),
        in_specs=[SMEM] + [VMEM] * len(weights),
        out_specs=VMEM,
        cost_estimate=pl.CostEstimate(flops=0, bytes_accessed=8 << 20, transcendentals=0),
        compiler_params=pltpu.CompilerParams(vmem_limit_bytes=12 << 20),
    )(flags, *weights)


def pack_phase(phase, flags, w_in, w_mid, w_out):
    ch = w_mid.shape[-1]
    outer = pack_weights(phase, ((0, 0), (0, ch)), flags, w_in)
    flags, _ = lax.optimization_barrier((flags, outer))
    return outer, pack_weights(phase, ((0, 0), (1, 0)), flags, w_mid, w_out)


def fields_of(refs):
    return [Field(refs[2 * i], refs[2 * i + 1]) for i in range(len(refs) // 2)]


def biases_of(direction, *refs):
    return [jnp.where(direction == 1, ref[1], ref[0]) for ref in refs]


def store_canonical(ref, flip, height, lo, hi, a, b, keep=None):
    for p in range(lo, hi):
        for o, v in ((0, a), (1, b)):
            i = 2 * p + o
            if i < height:
                at = jnp.where(flip, height - 1 - i, i)
                ref[at] = v[p - lo] if keep is None else jnp.where(keep, ref[at].astype(jnp.float32), v[p - lo].astype(jnp.float32)).astype(ref.dtype)


def first_kernel(height, flags, near_own, far_own, near_other, far_other, outer, inner, b_in, b_mid, b_out, state, result, *scratch):
    flip, own_first = flags[0] == 1, flags[1] == 1
    bias = biases_of(flags[2], b_in, b_mid, b_out)
    w_f, w_s, w_m, w_o = outer.at[0], outer.at[1], inner.at[0], inner.at[1]
    frame0, frame1, held, first0, middle0, first1, middle1 = fields = fields_of(scratch)
    for f in fields:
        f.clear()
    own, other = (near_own, far_own), (near_other, far_other)
    load_either(frame0, height + 6, flip, own_first, own, other, height)
    load_either(frame1, height + 3, flip, own_first, other, own, height)

    def emit_first(lo, hi, a, b):
        held.put_pairs(lo, hi, a.astype(jnp.float32), b.astype(jnp.float32))
        store_canonical(result, flip, height, lo, hi, a, b)

    def emit_second(lo, hi, a, b):
        for p in range(lo, hi):
            state[2 * p] = a[p - lo]
            state[2 * p + 1] = b[p - lo]
        store_canonical(result, flip, height, lo, hi, a, b, keep=own_first)

    def second_sums(lo, hi):
        return conv_pairs(frame1, w_f, lo, hi) + conv_pairs(held, w_s, lo, hi)

    n0, n1 = pair_sizes(height + 3), pair_sizes(height)
    frame0.zero_row(2 * n0[0])
    middle0.zero_row(2 * n0[2])
    first1.zero_row(2 * n1[0])
    run(
        frame_stages(lambda lo, hi: conv_pairs(frame0, w_f, lo, hi), n0, first0, middle0, w_m, w_o, *bias, emit_first)
        + frame_stages(second_sums, n1, first1, middle1, w_m, w_o, *bias, emit_second)
    )


def ahead_kernel(height, flags, near_own, far_own, near_other, far_other, outer, sums0, sums1, *scratch):
    flip, own_first = flags[0] == 1, flags[1] == 1
    frame0, frame1 = fields_of(scratch)
    for f in (frame0, frame1):
        f.clear()
    own, other = (near_own, far_own), (near_other, far_other)
    load_either(frame0, height + 6, flip, own_first, other, own, height)
    frame0.zero_row(2 * sums0.shape[0])
    load_either(frame1, height + 3, flip, own_first, own, other, height)
    for field, sums in ((frame0, sums0), (frame1, sums1)):
        sums[...] = conv_pairs(field, outer.at[0], 0, sums.shape[0])


def second_kernel(height, flags, near, far, sums0, sums1, outer, inner, b_in, b_mid, b_out, result, *scratch):
    flip, own_first = flags[0] == 1, flags[1] == 1
    bias = biases_of(1 - flags[2], b_in, b_mid, b_out)
    w_s, w_m, w_o = outer.at[1], inner.at[0], inner.at[1]
    state, held, first0, middle0, first1, middle1 = fields = fields_of(scratch)
    for f in fields:
        f.clear()
    depth = far.shape[0]
    for i in range(height):
        state.put_row(i, near[i])
    for i in range(depth):
        state.put_row(height + i, far[depth - 1 - i])
    state.zero_row(height + depth)

    def emit_first(lo, hi, a, b):
        held.put_pairs(lo, hi, a.astype(jnp.float32), b.astype(jnp.float32))
        store_canonical(result, flip, height, lo, hi, a, b)

    def emit_second(lo, hi, a, b):
        store_canonical(result, flip, height, lo, hi, a, b, keep=jnp.logical_not(own_first))

    n0, n1 = pair_sizes(height + 3), pair_sizes(height)
    middle0.zero_row(2 * n0[2])
    first1.zero_row(2 * n1[0])
    run(
        frame_stages(lambda lo, hi: sums0[lo:hi] + conv_pairs(state, w_s, lo, hi), n0, first0, middle0, w_m, w_o, *bias, emit_first)
        + frame_stages(lambda lo, hi: sums1[lo:hi] + conv_pairs(held, w_s, lo, hi), n1, first1, middle1, w_m, w_o, *bias, emit_second)
    )


VMEM = pl.BlockSpec(memory_space=pltpu.VMEM)
SMEM = pl.BlockSpec(memory_space=pltpu.SMEM)
LIMIT = 24 << 20


def field_scratch(count, rows, cols, ch):
    return [pltpu.VMEM((rows // 2 + 1, cols, 3 * ch), jnp.bfloat16) for _ in range(2 * count)]


def paired(features, w_in, b_in, w_mid, b_mid, w_out, b_out):
    _, _, slab, cols, ch = features.shape
    height = 2 * slab
    depth = 6
    where_row, owner = lax.axis_index("row"), lax.axis_index("frame")
    core, column = where_row % 2, where_row // 2
    own_first = ((owner == 0) | (owner == 3)).astype(jnp.int32)
    late = (owner >= 2).astype(jnp.int32)
    flags = jnp.stack([column, own_first, late])
    swap_core = [(0, 1), (1, 0), (2, 3), (3, 2)]
    swap_column = [(0, 2), (2, 0), (1, 3), (3, 1)]
    swap_near = [(0, 1), (1, 0), (2, 3), (3, 2)]
    cross = [(0, 2), (2, 0), (1, 3), (3, 1)]
    cross_both = [(4 * f + r, 4 * (f ^ 2) + (r ^ 2)) for f in range(4) for r in range(4)]
    swap_both = [(4 * f + r, 4 * (f ^ 1) + (r ^ 2)) for f in range(4) for r in range(4)]

    biases = (b_in, b_mid, b_out)
    mine = features[:, 0]
    kept = lax.dynamic_index_in_dim(mine, core, 0, keepdims=False)
    got = lax.ppermute(lax.dynamic_index_in_dim(mine, 1 - core, 0, keepdims=False), "row", swap_core)
    near_own = jnp.where(core == 0, jnp.concatenate([kept, got]), jnp.concatenate([got, kept]))
    edge = lax.dynamic_slice_in_dim(near_own, (height - depth) * (1 - column), depth, 0)
    near_other = lax.ppermute(near_own, "frame", swap_near)
    far_own = lax.ppermute(edge, "row", swap_column)
    far_other = lax.ppermute(edge, ("frame", "row"), swap_both)
    frames = (near_own, far_own, near_other, far_other)

    rows = height + 8
    bf16 = jnp.bfloat16
    cost = lambda rows: pl.CostEstimate(flops=rows * cols * ch * ch * 24, bytes_accessed=4 << 20, transcendentals=0)
    held_flags, _ = lax.optimization_barrier((flags, near_own))
    packed = pack_phase(0, held_flags, w_in, w_mid, w_out)
    state, early = pl.pallas_call(
        functools.partial(first_kernel, height),
        grid=(1,),
        out_shape=(
            jax.ShapeDtypeStruct((height, cols, ch), bf16),
            jax.ShapeDtypeStruct((height, cols, ch), bf16),
        ),
        in_specs=[SMEM] + [VMEM] * 9,
        out_specs=(VMEM, VMEM),
        scratch_shapes=field_scratch(7, rows, cols, ch),
        cost_estimate=cost(190),
        compiler_params=pltpu.CompilerParams(vmem_limit_bytes=LIMIT),
    )(flags, *frames, *packed, *biases)

    incoming = lax.ppermute(state, "frame", cross)
    edge = lax.ppermute(state[height - depth :], ("frame", "row"), cross_both)
    held_flags, _ = lax.optimization_barrier((flags, state))
    packed = pack_phase(1, held_flags, w_in, w_mid, w_out)
    sums = pl.pallas_call(
        functools.partial(ahead_kernel, height),
        grid=(1,),
        out_shape=tuple(jax.ShapeDtypeStruct((n, cols, 2 * ch), jnp.float32) for n in ((height + 6) // 2, (height + 3) // 2)),
        in_specs=[SMEM] + [VMEM] * 5,
        out_specs=(VMEM, VMEM),
        scratch_shapes=field_scratch(2, rows, cols, ch),
        cost_estimate=cost(42),
        compiler_params=pltpu.CompilerParams(vmem_limit_bytes=LIMIT),
    )(flags, *frames, packed[0])
    later = pl.pallas_call(
        functools.partial(second_kernel, height),
        grid=(1,),
        out_shape=jax.ShapeDtypeStruct((height, cols, ch), bf16),
        in_specs=[SMEM] + [VMEM] * 9,
        out_specs=VMEM,
        scratch_shapes=field_scratch(6, rows, cols, ch),
        cost_estimate=cost(120),
        compiler_params=pltpu.CompilerParams(vmem_limit_bytes=LIMIT),
    )(flags, incoming, edge, *sums, *packed, *biases)

    both = jnp.stack([early, later])
    kept = lax.dynamic_slice_in_dim(both, slab * core, slab, 1)
    got = lax.ppermute(lax.dynamic_slice_in_dim(both, slab * (1 - core), slab, 1), "row", swap_core)
    by_clip = jnp.where(core == 0, jnp.stack([kept, got], 1), jnp.stack([got, kept], 1))
    forward = jnp.where(late == 1, by_clip[1], by_clip[0])
    backward = jnp.where(late == 1, by_clip[0], by_clip[1])
    return forward[:, None], backward[:, None]


def with_halo(block, sides, width):
    for axis, dim in sides:
        count = lax.axis_size(axis)
        forward = [(i, i + 1) for i in range(count - 1)]
        backward = [(target, source) for source, target in forward]
        low = lax.ppermute(
            lax.slice_in_dim(block, block.shape[dim] - width, None, axis=dim), axis, forward
        )
        high = lax.ppermute(lax.slice_in_dim(block, 0, width, axis=dim), axis, backward)
        block = jnp.concatenate([low, block, high], axis=dim)
    return block


def shifted(shard, axis, by):
    length = lax.axis_size(axis)
    pairs = [(i, i + by) for i in range(length) if 0 <= i + by < length]
    return lax.ppermute(shard, axis, pairs)


def conv_layer(field, weight, bias_vec):
    padded = jnp.pad(field, ((0, 0), (1, 1), (0, 0)))
    row_count = padded.shape[0] - 2
    col_count = padded.shape[1] - 2
    summed = jnp.zeros((row_count, col_count, weight.shape[-1]), jnp.float32)
    for offset_y in range(3):
        for offset_x in range(3):
            window = padded[offset_y : offset_y + row_count, offset_x : offset_x + col_count, :]
            product = jnp.dot(
                window.reshape(row_count * col_count, window.shape[-1]),
                weight[offset_y, offset_x],
                preferred_element_type=jnp.float32,
            )
            summed = summed + product.reshape(row_count, col_count, weight.shape[-1])
    return summed + bias_vec


def activate(values):
    return jax.nn.gelu(values, approximate=False)


def pipelined(features, w_in, b_in, w_mid, b_mid, w_out, b_out):
    clip_count, frame_count, row_count, col_count, channels = features.shape
    owners = lax.axis_size("frame")
    owner_pos = lax.axis_index("frame")
    section_total = owners + clip_count - 1
    rim_depth = 3
    rimmed = with_halo(features, (("row", 2),), rim_depth)
    slab_start = lax.axis_index("row") * row_count
    total_rows = row_count * lax.axis_size("row")
    outer_rows = slab_start - 2 + jnp.arange(row_count + 4, dtype=jnp.int32)
    outer_mask = ((outer_rows >= 0) & (outer_rows < total_rows)).astype(jnp.float32)[:, None, None]
    inner_rows = slab_start - 1 + jnp.arange(row_count + 2, dtype=jnp.int32)
    inner_mask = ((inner_rows >= 0) & (inner_rows < total_rows)).astype(jnp.float32)[:, None, None]
    zero_state = jnp.zeros((row_count, col_count, channels), jnp.bfloat16)

    def skipped(operand):
        return zero_state

    def frame_step(frame_rim, carried, direction, is_live):
        state_rim = with_halo(carried, (("row", 0),), rim_depth)
        joined = jnp.concatenate([frame_rim, state_rim], axis=-1)

        def compute(joined_in):
            first_act = (
                activate(conv_layer(joined_in, w_in[direction], b_in[direction])) * outer_mask
            ).astype(jnp.bfloat16)
            middle = (
                activate(conv_layer(first_act, w_mid[direction], b_mid[direction])) * inner_mask
            ).astype(jnp.bfloat16)
            residual = first_act[2:-2].astype(jnp.float32)
            return (residual + conv_layer(middle, w_out[direction], b_out[direction])).astype(
                jnp.bfloat16
            )

        return lax.cond(is_live, compute, skipped, joined)

    def sweep_section(section_num, incoming, outputs, direction):
        position = owner_pos if direction == 0 else owners - 1 - owner_pos
        clip_index = section_num - position
        is_live = (clip_index >= 0) & (clip_index < clip_count)
        chosen = jnp.clip(clip_index, 0, clip_count - 1)
        clip_frames = lax.dynamic_index_in_dim(rimmed, chosen, 0, keepdims=False)
        clip_out = lax.dynamic_index_in_dim(outputs, chosen, 0, keepdims=False)
        carried = incoming
        frame_order = range(frame_count) if direction == 0 else range(frame_count - 1, -1, -1)
        for frame_slot in frame_order:
            carried = frame_step(clip_frames[frame_slot], carried, direction, is_live)
            clip_out = clip_out.at[frame_slot].set(
                jnp.where(is_live, carried, clip_out[frame_slot])
            )
        outputs = lax.dynamic_update_index_in_dim(outputs, clip_out, chosen, 0)
        if direction == 0:
            passed = shifted(carried, "frame", 1)
        else:
            passed = shifted(carried, "frame", -1)
        return (passed, outputs)

    blank_out = jnp.zeros_like(features)

    def forward_turn(section_num, carry):
        return sweep_section(section_num, carry[0], carry[1], 0)

    def backward_turn(section_num, carry):
        return sweep_section(section_num, carry[0], carry[1], 1)

    _, forward_states = lax.fori_loop(0, section_total, forward_turn, (zero_state, blank_out))
    _, backward_states = lax.fori_loop(0, section_total, backward_turn, (zero_state, blank_out))
    return (forward_states, backward_states)


def on_device(features, *weights):
    clips, frames, slab, _, _ = features.shape
    fits = (clips, frames, lax.axis_size("frame"), lax.axis_size("row")) == (2, 1, 4, 4) and slab >= 6
    return (paired if fits else pipelined)(features, *weights)


def solution(mesh):
    placed = (P("parts", "frame", "row", None, None), P(), P(), P(), P(), P(), P())

    return jax.shard_map(
        on_device,
        mesh=mesh,
        in_specs=placed,
        out_specs=(P("parts", "frame", "row", None, None), P("parts", "frame", "row", None, None)),
        check_vma=False,
    )
```

```python
import functools

import jax
import jax.numpy as jnp
from jax import lax
from jax.experimental import pallas as pl
from jax.experimental.pallas import tpu as pltpu
from jax.sharding import PartitionSpec as P


def gelu(v):
    return 0.5 * v * (1.0 + lax.erf(v * 0.7071067811865476))


def widen(rows):
    cols = rows.shape[1]
    col = lax.broadcasted_iota(jnp.int32, rows.shape, 1)
    left = jnp.where(col == 0, 0.0, pltpu.roll(rows, 1, 1))
    right = jnp.where(col == cols - 1, 0.0, pltpu.roll(rows, cols - 1, 1))
    return jnp.concatenate([left, rows, right], axis=-1).astype(jnp.bfloat16)


class Field:
    def __init__(self, even, odd):
        self.even, self.odd = even, odd

    def clear(self):
        self.odd[0] = jnp.zeros(self.odd.shape[1:], self.odd.dtype)

    def zero_row(self, row):
        self.even[row // 2] = jnp.zeros(self.even.shape[1:], self.even.dtype)

    def put_row(self, row, value):
        wide = widen(value.astype(jnp.float32)[None])[0]
        if row % 2 == 0:
            self.even[row // 2] = wide
        else:
            self.odd[row // 2 + 1] = wide

    def put_pairs(self, lo, hi, first, second):
        self.even[lo:hi] = widen(first)
        self.odd[lo + 1 : hi + 1] = widen(second)

    def patches(self, lo, hi):
        n = hi - lo
        cols, wide = self.even.shape[1:]
        parts = [self.odd[lo:hi], self.even[lo:hi], self.odd[lo + 1 : hi + 1], self.even[lo + 1 : hi + 1]]
        return jnp.concatenate(parts, axis=-1).reshape(n * cols, 4 * wide)

    def centre(self, lo, hi):
        ch = self.even.shape[2] // 3
        return (
            self.even[lo:hi, :, ch : 2 * ch].astype(jnp.float32),
            self.odd[lo + 1 : hi + 1, :, ch : 2 * ch].astype(jnp.float32),
        )


def conv_pairs(field, weight, lo, hi):
    out = jnp.dot(field.patches(lo, hi), weight[...], preferred_element_type=jnp.float32)
    return out.reshape(hi - lo, field.even.shape[1], weight.shape[-1])


def split(acc, bias):
    ch = acc.shape[-1] // 2
    return acc[:, :, :ch] + bias, acc[:, :, ch:] + bias


SPLIT = 7


def run(stages):
    waiting = []

    def finish_to(count):
        while len(waiting) > count:
            done = waiting.pop(0)
            done[0](*done[1:])

    for s, (pairs, sums, finish) in enumerate(stages):
        edge = min(max(SPLIT - s, 0), pairs)
        if edge == 0 or edge == pairs:
            finish_to(0)
            waiting.append((finish, 0, pairs, sums(0, pairs)))
            continue
        finish_to(1)
        waiting.append((finish, 0, edge, sums(0, edge)))
        finish_to(1)
        waiting.append((finish, edge, pairs, sums(edge, pairs)))
    finish_to(0)


def frame_stages(first_sums, sizes, first, middle, w_mid, w_out, b_in, b_mid, b_out, emit):
    def activated(field, bias):
        def finish(lo, hi, acc):
            a, b = split(acc, bias)
            field.put_pairs(lo, hi, gelu(a), gelu(b))

        return finish

    def add(lo, hi, acc):
        a, b = split(acc, b_out)
        ra, rb = first.centre(lo, hi)
        emit(lo, hi, (ra + a).astype(jnp.bfloat16), (rb + b).astype(jnp.bfloat16))

    return [
        (sizes[0], first_sums, activated(first, b_in)),
        (sizes[1], lambda lo, hi: conv_pairs(first, w_mid, lo, hi), activated(middle, b_mid)),
        (sizes[2], lambda lo, hi: conv_pairs(middle, w_out, lo, hi), add),
    ]


def pair_sizes(rows):
    return (rows + 3) // 2, (rows + 2) // 2, (rows + 1) // 2


def load_either(field, rows, flip, pick, a, b, height):
    depth = a[1].shape[0]
    for i in range(rows):
        if i < height:
            at, k = jnp.where(flip, height - 1 - i, i), 0
        else:
            at, k = jnp.where(flip, depth - 1 - (i - height), i - height), 1
        field.put_row(i, jnp.where(pick, a[k][at].astype(jnp.float32), b[k][at].astype(jnp.float32)))


def pack_kernel(phase, parts, flags, *refs):
    flip = flags[0] == 1
    direction = flags[2] if phase == 0 else 1 - flags[2]
    packed = refs[-1]
    ch = packed.shape[-1] // 2
    zero = jnp.zeros((3 * ch, ch), packed.dtype)
    for conv, (which, base) in enumerate(parts):
        packed[conv, 9 * ch : 12 * ch, :ch] = zero
        packed[conv, : 3 * ch, ch:] = zero
        for dy in range(3):
            at = jnp.where(flip, 2 - dy, dy)
            for dx in range(3):
                taps = refs[which][direction, at, dx, base : base + ch, :]
                for o in range(2):
                    row = 3 * ch * (dy + o) + ch * dx
                    packed[conv, row : row + ch, o * ch : (o + 1) * ch] = taps


def pack_weights(phase, parts, flags, *weights):
    ch = weights[0].shape[-1]
    return pl.pallas_call(
        functools.partial(pack_kernel, phase, parts),
        out_shape=jax.ShapeDtypeStruct((len(parts), 12 * ch, 2 * ch), weights[0].dtype),
        in_specs=[SMEM] + [VMEM] * len(weights),
        out_specs=VMEM,
        cost_estimate=pl.CostEstimate(flops=0, bytes_accessed=8 << 20, transcendentals=0),
        compiler_params=pltpu.CompilerParams(vmem_limit_bytes=12 << 20),
    )(flags, *weights)


def pack_outer(phase, flags, w_in):
    return pack_weights(phase, ((0, 0), (0, w_in.shape[-1])), flags, w_in)


def pack_inner(phase, flags, outer, w_mid, w_out):
    flags, _ = lax.optimization_barrier((flags, outer))
    return pack_weights(phase, ((0, 0), (1, 0)), flags, w_mid, w_out)


def fields_of(refs):
    return [Field(refs[2 * i], refs[2 * i + 1]) for i in range(len(refs) // 2)]


def biases_of(direction, *refs):
    return [jnp.where(direction == 1, ref[1], ref[0]) for ref in refs]


def store_canonical(ref, flip, height, lo, hi, a, b, keep=None):
    for p in range(lo, hi):
        for o, v in ((0, a), (1, b)):
            i = 2 * p + o
            if i < height:
                at = jnp.where(flip, height - 1 - i, i)
                ref[at] = v[p - lo] if keep is None else jnp.where(keep, ref[at].astype(jnp.float32), v[p - lo].astype(jnp.float32)).astype(ref.dtype)


def first_kernel(height, flags, near_own, far_own, near_other, far_other, outer, inner, b_in, b_mid, b_out, state, edge, result, *scratch):
    flip, own_first = flags[0] == 1, flags[1] == 1
    bias = biases_of(flags[2], b_in, b_mid, b_out)
    w_f, w_s, w_m, w_o = outer.at[0], outer.at[1], inner.at[0], inner.at[1]
    frame0, frame1, held, first0, middle0, first1, middle1 = fields = fields_of(scratch)
    for f in fields:
        f.clear()
    own, other = (near_own, far_own), (near_other, far_other)
    load_either(frame0, height + 6, flip, own_first, own, other, height)
    load_either(frame1, height + 3, flip, own_first, other, own, height)

    def emit_first(lo, hi, a, b):
        held.put_pairs(lo, hi, a.astype(jnp.float32), b.astype(jnp.float32))
        store_canonical(result, flip, height, lo, hi, a, b)

    def emit_second(lo, hi, a, b):
        for p in range(lo, hi):
            for i, v in ((2 * p, a[p - lo]), (2 * p + 1, b[p - lo])):
                state[i] = v
                if i >= height - edge.shape[0]:
                    edge[i - (height - edge.shape[0])] = v
        store_canonical(result, flip, height, lo, hi, a, b, keep=own_first)

    def second_sums(lo, hi):
        return conv_pairs(frame1, w_f, lo, hi) + conv_pairs(held, w_s, lo, hi)

    n0, n1 = pair_sizes(height + 3), pair_sizes(height)
    frame0.zero_row(2 * n0[0])
    middle0.zero_row(2 * n0[2])
    first1.zero_row(2 * n1[0])
    run(
        frame_stages(lambda lo, hi: conv_pairs(frame0, w_f, lo, hi), n0, first0, middle0, w_m, w_o, *bias, emit_first)
        + frame_stages(second_sums, n1, first1, middle1, w_m, w_o, *bias, emit_second)
    )


def ahead_kernel(height, flags, near_own, far_own, near_other, far_other, outer, sums0, sums1, *scratch):
    flip, own_first = flags[0] == 1, flags[1] == 1
    frame0, frame1 = fields_of(scratch)
    for f in (frame0, frame1):
        f.clear()
    own, other = (near_own, far_own), (near_other, far_other)
    load_either(frame0, height + 6, flip, own_first, other, own, height)
    frame0.zero_row(2 * sums0.shape[0])
    load_either(frame1, height + 3, flip, own_first, own, other, height)
    for field, sums in ((frame0, sums0), (frame1, sums1)):
        sums[...] = conv_pairs(field, outer.at[0], 0, sums.shape[0])


def second_kernel(height, flags, near_a, far_a, near_b, far_b, sums0, sums1, outer, inner, b_in, b_mid, b_out, result, *scratch):
    flip, own_first = flags[0] == 1, flags[1] == 1
    bias = biases_of(1 - flags[2], b_in, b_mid, b_out)
    w_s, w_m, w_o = outer.at[1], inner.at[0], inner.at[1]
    state, held, first0, middle0, first1, middle1 = fields = fields_of(scratch)
    for f in fields:
        f.clear()
    depth = far_a.shape[0]
    for i in range(height + depth):
        a, b, at = (near_a, near_b, i) if i < height else (far_a, far_b, height + depth - 1 - i)
        state.put_row(i, jnp.where(own_first, a[at].astype(jnp.float32), b[at].astype(jnp.float32)))
    state.zero_row(height + depth)

    def emit_first(lo, hi, a, b):
        held.put_pairs(lo, hi, a.astype(jnp.float32), b.astype(jnp.float32))
        store_canonical(result, flip, height, lo, hi, a, b)

    def emit_second(lo, hi, a, b):
        store_canonical(result, flip, height, lo, hi, a, b)

    n0, n1 = pair_sizes(height + 3), pair_sizes(height)
    middle0.zero_row(2 * n0[2])
    run(frame_stages(lambda lo, hi: sums0[lo:hi] + conv_pairs(state, w_s, lo, hi), n0, first0, middle0, w_m, w_o, *bias, emit_first))

    @pl.when(own_first)
    def _():
        first1.zero_row(2 * n1[0])
        run(frame_stages(lambda lo, hi: sums1[lo:hi] + conv_pairs(held, w_s, lo, hi), n1, first1, middle1, w_m, w_o, *bias, emit_second))


VMEM = pl.BlockSpec(memory_space=pltpu.VMEM)
SMEM = pl.BlockSpec(memory_space=pltpu.SMEM)
LIMIT = 14 << 20


def field_scratch(count, rows, cols, ch):
    return [pltpu.VMEM((rows // 2 + 1, cols, 3 * ch), jnp.bfloat16) for _ in range(2 * count)]


def paired(features, w_in, b_in, w_mid, b_mid, w_out, b_out):
    _, _, slab, cols, ch = features.shape
    height = 2 * slab
    depth = 6
    where_row, owner = lax.axis_index("row"), lax.axis_index("frame")
    core, column = where_row % 2, where_row // 2
    own_first = ((owner == 0) | (owner == 3)).astype(jnp.int32)
    late = (owner >= 2).astype(jnp.int32)
    flags = jnp.stack([column, own_first, late])
    swap_core = [(0, 1), (1, 0), (2, 3), (3, 2)]
    swap_column = [(0, 2), (2, 0), (1, 3), (3, 1)]
    swap_near = [(0, 1), (1, 0), (2, 3), (3, 2)]
    outer_cross, inner_cross = (1, 3, 0, 2), (None, 2, 1, None)

    def crossing(targets, mirror):
        pairs = []
        for f in range(4):
            for r in range(4):
                stays = targets[f] is None
                pairs.append((4 * f + r, 4 * f + (r ^ 1) if stays else 4 * targets[f] + (r ^ mirror)))
        return pairs

    swap_both = [(4 * f + r, 4 * (f ^ 1) + (r ^ 2)) for f in range(4) for r in range(4)]

    biases = (b_in, b_mid, b_out)
    mine = features[:, 0]
    kept = lax.dynamic_index_in_dim(mine, core, 0, keepdims=False)
    got = lax.ppermute(lax.dynamic_index_in_dim(mine, 1 - core, 0, keepdims=False), "row", swap_core)
    near_own = jnp.where(core == 0, jnp.concatenate([kept, got]), jnp.concatenate([got, kept]))
    edge = lax.dynamic_slice_in_dim(near_own, (height - depth) * (1 - column), depth, 0)
    near_other = lax.ppermute(near_own, "frame", swap_near)
    far_own = lax.ppermute(edge, "row", swap_column)
    far_other = lax.ppermute(edge, ("frame", "row"), swap_both)
    frames = (near_own, far_own, near_other, far_other)

    rows = height + 8
    bf16 = jnp.bfloat16
    cost = lambda rows: pl.CostEstimate(flops=rows * cols * ch * ch * 24, bytes_accessed=4 << 20, transcendentals=0)
    held_flags, _ = lax.optimization_barrier((flags, near_own))
    outer = pack_outer(0, held_flags, w_in)
    packed = outer, pack_inner(0, held_flags, outer, w_mid, w_out)
    state, edge, early = pl.pallas_call(
        functools.partial(first_kernel, height),
        grid=(1,),
        out_shape=(
            jax.ShapeDtypeStruct((height, cols, ch), bf16),
            jax.ShapeDtypeStruct((depth, cols, ch), bf16),
            jax.ShapeDtypeStruct((height, cols, ch), bf16),
        ),
        in_specs=[SMEM] + [VMEM] * 9,
        out_specs=(VMEM, VMEM, VMEM),
        scratch_shapes=field_scratch(7, rows, cols, ch),
        cost_estimate=cost(190),
        compiler_params=pltpu.CompilerParams(vmem_limit_bytes=LIMIT),
    )(flags, *frames, *packed, *biases)

    handed = []
    for targets in (outer_cross, inner_cross):
        for rows_of, mirror in ((state, 0), (edge, 2)):
            handed.append(lax.ppermute(rows_of, ("frame", "row"), crossing(targets, mirror)))
    held_flags, _ = lax.optimization_barrier((flags, state))
    outer = pack_outer(1, held_flags, w_in)
    packed = outer, pack_inner(1, held_flags, outer, w_mid, w_out)
    ahead = pl.pallas_call(
        functools.partial(ahead_kernel, height),
        grid=(1,),
        out_shape=tuple(jax.ShapeDtypeStruct((n, cols, 2 * ch), jnp.float32) for n in ((height + 6) // 2, (height + 3) // 2)),
        in_specs=[SMEM] + [VMEM] * 5,
        out_specs=(VMEM, VMEM),
        scratch_shapes=field_scratch(2, rows, cols, ch),
        cost_estimate=cost(42),
        compiler_params=pltpu.CompilerParams(vmem_limit_bytes=LIMIT),
    )
    sums = ahead(flags, *frames, packed[0])
    later = pl.pallas_call(
        functools.partial(second_kernel, height),
        grid=(1,),
        out_shape=jax.ShapeDtypeStruct((height, cols, ch), bf16),
        in_specs=[SMEM] + [VMEM] * 11,
        out_specs=VMEM,
        scratch_shapes=field_scratch(6, rows, cols, ch),
        cost_estimate=cost(120),
        compiler_params=pltpu.CompilerParams(vmem_limit_bytes=LIMIT),
    )(flags, *handed, *sums, *packed, *biases)

    both = jnp.stack([early, later])
    kept = lax.dynamic_slice_in_dim(both, slab * core, slab, 1)
    got = lax.ppermute(lax.dynamic_slice_in_dim(both, slab * (1 - core), slab, 1), "row", swap_core)
    by_clip = jnp.where(core == 0, jnp.stack([kept, got], 1), jnp.stack([got, kept], 1))
    forward = jnp.where(late == 1, by_clip[1], by_clip[0])
    backward = jnp.where(late == 1, by_clip[0], by_clip[1])
    return forward[:, None], backward[:, None]


def with_halo(block, sides, width):
    for axis, dim in sides:
        count = lax.axis_size(axis)
        forward = [(i, i + 1) for i in range(count - 1)]
        backward = [(target, source) for source, target in forward]
        low = lax.ppermute(
            lax.slice_in_dim(block, block.shape[dim] - width, None, axis=dim), axis, forward
        )
        high = lax.ppermute(lax.slice_in_dim(block, 0, width, axis=dim), axis, backward)
        block = jnp.concatenate([low, block, high], axis=dim)
    return block


def shifted(shard, axis, by):
    length = lax.axis_size(axis)
    pairs = [(i, i + by) for i in range(length) if 0 <= i + by < length]
    return lax.ppermute(shard, axis, pairs)


def conv_layer(field, weight, bias_vec):
    padded = jnp.pad(field, ((0, 0), (1, 1), (0, 0)))
    row_count = padded.shape[0] - 2
    col_count = padded.shape[1] - 2
    summed = jnp.zeros((row_count, col_count, weight.shape[-1]), jnp.float32)
    for offset_y in range(3):
        for offset_x in range(3):
            window = padded[offset_y : offset_y + row_count, offset_x : offset_x + col_count, :]
            product = jnp.dot(
                window.reshape(row_count * col_count, window.shape[-1]),
                weight[offset_y, offset_x],
                preferred_element_type=jnp.float32,
            )
            summed = summed + product.reshape(row_count, col_count, weight.shape[-1])
    return summed + bias_vec


def activate(values):
    return jax.nn.gelu(values, approximate=False)


def pipelined(features, w_in, b_in, w_mid, b_mid, w_out, b_out):
    clip_count, frame_count, row_count, col_count, channels = features.shape
    owners = lax.axis_size("frame")
    owner_pos = lax.axis_index("frame")
    section_total = owners + clip_count - 1
    rim_depth = 3
    rimmed = with_halo(features, (("row", 2),), rim_depth)
    slab_start = lax.axis_index("row") * row_count
    total_rows = row_count * lax.axis_size("row")
    outer_rows = slab_start - 2 + jnp.arange(row_count + 4, dtype=jnp.int32)
    outer_mask = ((outer_rows >= 0) & (outer_rows < total_rows)).astype(jnp.float32)[:, None, None]
    inner_rows = slab_start - 1 + jnp.arange(row_count + 2, dtype=jnp.int32)
    inner_mask = ((inner_rows >= 0) & (inner_rows < total_rows)).astype(jnp.float32)[:, None, None]
    zero_state = jnp.zeros((row_count, col_count, channels), jnp.bfloat16)

    def skipped(operand):
        return zero_state

    def frame_step(frame_rim, carried, direction, is_live):
        state_rim = with_halo(carried, (("row", 0),), rim_depth)
        joined = jnp.concatenate([frame_rim, state_rim], axis=-1)

        def compute(joined_in):
            first_act = (
                activate(conv_layer(joined_in, w_in[direction], b_in[direction])) * outer_mask
            ).astype(jnp.bfloat16)
            middle = (
                activate(conv_layer(first_act, w_mid[direction], b_mid[direction])) * inner_mask
            ).astype(jnp.bfloat16)
            residual = first_act[2:-2].astype(jnp.float32)
            return (residual + conv_layer(middle, w_out[direction], b_out[direction])).astype(
                jnp.bfloat16
            )

        return lax.cond(is_live, compute, skipped, joined)

    def sweep_section(section_num, incoming, outputs, direction):
        position = owner_pos if direction == 0 else owners - 1 - owner_pos
        clip_index = section_num - position
        is_live = (clip_index >= 0) & (clip_index < clip_count)
        chosen = jnp.clip(clip_index, 0, clip_count - 1)
        clip_frames = lax.dynamic_index_in_dim(rimmed, chosen, 0, keepdims=False)
        clip_out = lax.dynamic_index_in_dim(outputs, chosen, 0, keepdims=False)
        carried = incoming
        frame_order = range(frame_count) if direction == 0 else range(frame_count - 1, -1, -1)
        for frame_slot in frame_order:
            carried = frame_step(clip_frames[frame_slot], carried, direction, is_live)
            clip_out = clip_out.at[frame_slot].set(
                jnp.where(is_live, carried, clip_out[frame_slot])
            )
        outputs = lax.dynamic_update_index_in_dim(outputs, clip_out, chosen, 0)
        if direction == 0:
            passed = shifted(carried, "frame", 1)
        else:
            passed = shifted(carried, "frame", -1)
        return (passed, outputs)

    blank_out = jnp.zeros_like(features)

    def forward_turn(section_num, carry):
        return sweep_section(section_num, carry[0], carry[1], 0)

    def backward_turn(section_num, carry):
        return sweep_section(section_num, carry[0], carry[1], 1)

    _, forward_states = lax.fori_loop(0, section_total, forward_turn, (zero_state, blank_out))
    _, backward_states = lax.fori_loop(0, section_total, backward_turn, (zero_state, blank_out))
    return (forward_states, backward_states)


def on_device(features, *weights):
    clips, frames, slab, _, _ = features.shape
    fits = (clips, frames, lax.axis_size("frame"), lax.axis_size("row")) == (2, 1, 4, 4) and slab >= 6
    return (paired if fits else pipelined)(features, *weights)


def solution(mesh):
    placed = (P("parts", "frame", "row", None, None), P(), P(), P(), P(), P(), P())

    return jax.shard_map(
        on_device,
        mesh=mesh,
        in_specs=placed,
        out_specs=(P("parts", "frame", "row", None, None), P("parts", "frame", "row", None, None)),
        check_vma=False,
    )
```

```python
import functools

import jax
import jax.numpy as jnp
from jax import lax
from jax.experimental import pallas as pl
from jax.experimental.pallas import tpu as pltpu
from jax.sharding import PartitionSpec as P


def gelu(v):
    return 0.5 * v * (1.0 + lax.erf(v * 0.7071067811865476))


class Field:
    def __init__(self, even, odd, wide_even, wide_odd):
        self.even, self.odd = even, odd
        self.wide = wide_even, wide_odd

    def clear(self):
        self.odd[0] = jnp.zeros(self.odd.shape[1:], self.odd.dtype)
        for wide in self.wide:
            n, cols, ch = wide.shape
            wide[:, :8, :] = jnp.zeros((n, 8, ch), wide.dtype)
            wide[:, cols - 8 :, :] = jnp.zeros((n, 8, ch), wide.dtype)

    def widened(self, k, lo, hi, rows):
        wide = self.wide[k]
        cols = rows.shape[1]
        wide[lo:hi, 8 : 8 + cols, :] = rows
        left, right = wide[lo:hi, 7 : 7 + cols, :], wide[lo:hi, 9 : 9 + cols, :]
        return jnp.concatenate([left, rows, right], axis=-1).astype(jnp.bfloat16)

    def zero_row(self, row):
        self.even[row // 2] = jnp.zeros(self.even.shape[1:], self.even.dtype)

    def put_row(self, row, value):
        wide = self.widened(row % 2, row // 2, row // 2 + 1, value.astype(jnp.float32)[None])[0]
        if row % 2 == 0:
            self.even[row // 2] = wide
        else:
            self.odd[row // 2 + 1] = wide

    def put_pairs(self, lo, hi, first, second):
        self.even[lo:hi] = self.widened(0, lo, hi, first)
        self.odd[lo + 1 : hi + 1] = self.widened(1, lo, hi, second)

    def patches(self, lo, hi):
        n = hi - lo
        cols, wide = self.even.shape[1:]
        parts = [self.odd[lo:hi], self.even[lo:hi], self.odd[lo + 1 : hi + 1], self.even[lo + 1 : hi + 1]]
        return jnp.concatenate(parts, axis=-1).reshape(n * cols, 4 * wide)

    def centre(self, lo, hi):
        ch = self.even.shape[2] // 3
        return (
            self.even[lo:hi, :, ch : 2 * ch].astype(jnp.float32),
            self.odd[lo + 1 : hi + 1, :, ch : 2 * ch].astype(jnp.float32),
        )


def conv_pairs(field, weight, lo, hi):
    out = jnp.dot(field.patches(lo, hi), weight[...], preferred_element_type=jnp.float32)
    return out.reshape(hi - lo, field.even.shape[1], weight.shape[-1])


def split(acc, bias):
    ch = acc.shape[-1] // 2
    return acc[:, :, :ch] + bias, acc[:, :, ch:] + bias


def run(stages, split):
    waiting = []

    def finish_to(count):
        while len(waiting) > count:
            done = waiting.pop(0)
            done[0](*done[1:])

    for s, (pairs, sums, finish) in enumerate(stages):
        edge = min(max(split - s, 0), pairs)
        if edge == 0 or edge == pairs:
            finish_to(0)
            waiting.append((finish, 0, pairs, sums(0, pairs)))
            continue
        finish_to(1)
        waiting.append((finish, 0, edge, sums(0, edge)))
        finish_to(1)
        waiting.append((finish, edge, pairs, sums(edge, pairs)))
    finish_to(0)


def frame_stages(first_sums, sizes, first, middle, w_mid, w_out, b_in, b_mid, b_out, emit):
    def activated(field, bias):
        def finish(lo, hi, acc):
            a, b = split(acc, bias)
            field.put_pairs(lo, hi, gelu(a), gelu(b))

        return finish

    def add(lo, hi, acc):
        a, b = split(acc, b_out)
        ra, rb = first.centre(lo, hi)
        emit(lo, hi, (ra + a).astype(jnp.bfloat16), (rb + b).astype(jnp.bfloat16))

    return [
        (sizes[0], first_sums, activated(first, b_in)),
        (sizes[1], lambda lo, hi: conv_pairs(first, w_mid, lo, hi), activated(middle, b_mid)),
        (sizes[2], lambda lo, hi: conv_pairs(middle, w_out, lo, hi), add),
    ]


def pair_sizes(rows):
    return (rows + 3) // 2, (rows + 2) // 2, (rows + 1) // 2


def load_either(field, rows, flip, pick, a, b, height):
    depth = a[1].shape[0]
    for i in range(rows):
        if i < height:
            at, k = jnp.where(flip, height - 1 - i, i), 0
        else:
            at, k = jnp.where(flip, depth - 1 - (i - height), i - height), 1
        field.put_row(i, jnp.where(pick, a[k][at].astype(jnp.float32), b[k][at].astype(jnp.float32)))


def pack_kernel(phase, parts, flags, *refs):
    flip = flags[0] == 1
    direction = flags[2] if phase == 0 else 1 - flags[2]
    packed = refs[-1]
    ch = packed.shape[-1] // 2
    zero = jnp.zeros((3 * ch, ch), packed.dtype)
    for conv, (which, base) in enumerate(parts):
        packed[conv, 9 * ch : 12 * ch, :ch] = zero
        packed[conv, : 3 * ch, ch:] = zero
        for dy in range(3):
            at = jnp.where(flip, 2 - dy, dy)
            for dx in range(3):
                taps = refs[which][direction, at, dx, base : base + ch, :]
                for o in range(2):
                    row = 3 * ch * (dy + o) + ch * dx
                    packed[conv, row : row + ch, o * ch : (o + 1) * ch] = taps


def pack_weights(phase, parts, flags, *weights):
    ch = weights[0].shape[-1]
    return pl.pallas_call(
        functools.partial(pack_kernel, phase, parts),
        out_shape=jax.ShapeDtypeStruct((len(parts), 12 * ch, 2 * ch), weights[0].dtype),
        in_specs=[SMEM] + [VMEM] * len(weights),
        out_specs=VMEM,
        cost_estimate=pl.CostEstimate(flops=0, bytes_accessed=8 << 20, transcendentals=0),
        compiler_params=pltpu.CompilerParams(vmem_limit_bytes=12 << 20),
    )(flags, *weights)


def pack_outer(phase, flags, w_in):
    return pack_weights(phase, ((0, 0), (0, w_in.shape[-1])), flags, w_in)


def pack_inner(phase, flags, outer, w_mid, w_out):
    flags, _ = lax.optimization_barrier((flags, outer))
    return pack_weights(phase, ((0, 0), (1, 0)), flags, w_mid, w_out)


def fields_of(refs):
    return [Field(*refs[4 * i : 4 * i + 4]) for i in range(len(refs) // 4)]


def biases_of(direction, *refs):
    return [jnp.where(direction == 1, ref[1], ref[0]) for ref in refs]


def store_canonical(ref, flip, height, lo, hi, a, b, keep=None):
    for p in range(lo, hi):
        for o, v in ((0, a), (1, b)):
            i = 2 * p + o
            if i < height:
                at = jnp.where(flip, height - 1 - i, i)
                ref[at] = v[p - lo] if keep is None else jnp.where(keep, ref[at].astype(jnp.float32), v[p - lo].astype(jnp.float32)).astype(ref.dtype)


def first_kernel(height, flags, near_own, far_own, near_other, far_other, outer, inner, b_in, b_mid, b_out, state, edge, result, *scratch):
    flip, own_first = flags[0] == 1, flags[1] == 1
    bias = biases_of(flags[2], b_in, b_mid, b_out)
    w_f, w_s, w_m, w_o = outer.at[0], outer.at[1], inner.at[0], inner.at[1]
    frame0, frame1, held, first0, middle0, first1, middle1 = fields = fields_of(scratch)
    for f in fields:
        f.clear()
    own, other = (near_own, far_own), (near_other, far_other)
    load_either(frame0, height + 6, flip, own_first, own, other, height)
    load_either(frame1, height + 3, flip, own_first, other, own, height)

    def emit_first(lo, hi, a, b):
        held.put_pairs(lo, hi, a.astype(jnp.float32), b.astype(jnp.float32))
        store_canonical(result, flip, height, lo, hi, a, b)

    def emit_second(lo, hi, a, b):
        for p in range(lo, hi):
            for i, v in ((2 * p, a[p - lo]), (2 * p + 1, b[p - lo])):
                state[i] = v
                if i >= height - edge.shape[0]:
                    edge[i - (height - edge.shape[0])] = v
        store_canonical(result, flip, height, lo, hi, a, b, keep=own_first)

    def second_sums(lo, hi):
        return conv_pairs(frame1, w_f, lo, hi) + conv_pairs(held, w_s, lo, hi)

    n0, n1 = pair_sizes(height + 3), pair_sizes(height)
    frame0.zero_row(2 * n0[0])
    middle0.zero_row(2 * n0[2])
    first1.zero_row(2 * n1[0])
    run(
        frame_stages(lambda lo, hi: conv_pairs(frame0, w_f, lo, hi), n0, first0, middle0, w_m, w_o, *bias, emit_first)
        + frame_stages(second_sums, n1, first1, middle1, w_m, w_o, *bias, emit_second),
        8,
    )


def ahead_kernel(height, flags, near_own, far_own, near_other, far_other, outer, sums0, sums1, *scratch):
    flip, own_first = flags[0] == 1, flags[1] == 1
    frame0, frame1 = fields_of(scratch)
    for f in (frame0, frame1):
        f.clear()
    own, other = (near_own, far_own), (near_other, far_other)
    load_either(frame0, height + 6, flip, own_first, other, own, height)
    frame0.zero_row(2 * sums0.shape[0])
    load_either(frame1, height + 3, flip, own_first, own, other, height)
    for field, sums in ((frame0, sums0), (frame1, sums1)):
        sums[...] = conv_pairs(field, outer.at[0], 0, sums.shape[0])


def second_kernel(height, flags, near_a, far_a, near_b, far_b, sums0, sums1, outer, inner, b_in, b_mid, b_out, result, *scratch):
    flip, own_first = flags[0] == 1, flags[1] == 1
    bias = biases_of(1 - flags[2], b_in, b_mid, b_out)
    w_s, w_m, w_o = outer.at[1], inner.at[0], inner.at[1]
    state, held, first0, middle0, first1, middle1 = fields = fields_of(scratch)
    for f in fields:
        f.clear()
    depth = far_a.shape[0]
    for i in range(height + depth):
        a, b, at = (near_a, near_b, i) if i < height else (far_a, far_b, height + depth - 1 - i)
        state.put_row(i, jnp.where(own_first, a[at].astype(jnp.float32), b[at].astype(jnp.float32)))
    state.zero_row(height + depth)

    def emit_first(lo, hi, a, b):
        held.put_pairs(lo, hi, a.astype(jnp.float32), b.astype(jnp.float32))
        store_canonical(result, flip, height, lo, hi, a, b)

    def emit_second(lo, hi, a, b):
        store_canonical(result, flip, height, lo, hi, a, b)

    n0, n1 = pair_sizes(height + 3), pair_sizes(height)
    middle0.zero_row(2 * n0[2])
    run(frame_stages(lambda lo, hi: sums0[lo:hi] + conv_pairs(state, w_s, lo, hi), n0, first0, middle0, w_m, w_o, *bias, emit_first), 7)

    @pl.when(own_first)
    def _():
        first1.zero_row(2 * n1[0])
        run(frame_stages(lambda lo, hi: sums1[lo:hi] + conv_pairs(held, w_s, lo, hi), n1, first1, middle1, w_m, w_o, *bias, emit_second), 7)


VMEM = pl.BlockSpec(memory_space=pltpu.VMEM)
SMEM = pl.BlockSpec(memory_space=pltpu.SMEM)
LIMIT = 14 << 20


def field_scratch(count, rows, cols, ch):
    wide = pltpu.VMEM((rows // 2 + 1, cols, 3 * ch), jnp.bfloat16)
    padded = pltpu.VMEM((rows // 2, cols + 16, ch), jnp.float32)
    return [wide, wide, padded, padded] * count


def paired(features, w_in, b_in, w_mid, b_mid, w_out, b_out):
    _, _, slab, cols, ch = features.shape
    height = 2 * slab
    depth = 6
    where_row, owner = lax.axis_index("row"), lax.axis_index("frame")
    core, column = where_row % 2, where_row // 2
    own_first = ((owner == 0) | (owner == 3)).astype(jnp.int32)
    late = (owner >= 2).astype(jnp.int32)
    flags = jnp.stack([column, own_first, late])
    swap_core = [(0, 1), (1, 0), (2, 3), (3, 2)]
    swap_column = [(0, 2), (2, 0), (1, 3), (3, 1)]
    swap_near = [(0, 1), (1, 0), (2, 3), (3, 2)]
    outer_cross, inner_cross = (1, 3, 0, 2), (None, 2, 1, None)

    def crossing(targets, mirror):
        pairs = []
        for f in range(4):
            for r in range(4):
                stays = targets[f] is None
                pairs.append((4 * f + r, 4 * f + (r ^ 1) if stays else 4 * targets[f] + (r ^ mirror)))
        return pairs

    swap_both = [(4 * f + r, 4 * (f ^ 1) + (r ^ 2)) for f in range(4) for r in range(4)]

    biases = (b_in, b_mid, b_out)
    mine = features[:, 0]
    kept = lax.dynamic_index_in_dim(mine, core, 0, keepdims=False)
    got = lax.ppermute(lax.dynamic_index_in_dim(mine, 1 - core, 0, keepdims=False), "row", swap_core)
    near_own = jnp.where(core == 0, jnp.concatenate([kept, got]), jnp.concatenate([got, kept]))
    edge = lax.dynamic_slice_in_dim(near_own, (height - depth) * (1 - column), depth, 0)
    near_other = lax.ppermute(near_own, "frame", swap_near)
    far_own = lax.ppermute(edge, "row", swap_column)
    far_other = lax.ppermute(edge, ("frame", "row"), swap_both)
    frames = (near_own, far_own, near_other, far_other)

    rows = height + 8
    bf16 = jnp.bfloat16
    cost = lambda rows: pl.CostEstimate(flops=rows * cols * ch * ch * 24, bytes_accessed=4 << 20, transcendentals=0)
    held_flags, _ = lax.optimization_barrier((flags, near_own))
    outer = pack_outer(0, held_flags, w_in)
    packed = outer, pack_inner(0, held_flags, outer, w_mid, w_out)
    state, edge, early = pl.pallas_call(
        functools.partial(first_kernel, height),
        grid=(1,),
        out_shape=(
            jax.ShapeDtypeStruct((height, cols, ch), bf16),
            jax.ShapeDtypeStruct((depth, cols, ch), bf16),
            jax.ShapeDtypeStruct((height, cols, ch), bf16),
        ),
        in_specs=[SMEM] + [VMEM] * 9,
        out_specs=(VMEM, VMEM, VMEM),
        scratch_shapes=field_scratch(7, rows, cols, ch),
        cost_estimate=cost(190),
        compiler_params=pltpu.CompilerParams(vmem_limit_bytes=LIMIT),
    )(flags, *frames, *packed, *biases)

    handed = []
    for targets in (outer_cross, inner_cross):
        for rows_of, mirror in ((state, 0), (edge, 2)):
            handed.append(lax.ppermute(rows_of, ("frame", "row"), crossing(targets, mirror)))
    held_flags, _ = lax.optimization_barrier((flags, state))
    outer = pack_outer(1, held_flags, w_in)
    packed = outer, pack_inner(1, held_flags, outer, w_mid, w_out)
    ahead = pl.pallas_call(
        functools.partial(ahead_kernel, height),
        grid=(1,),
        out_shape=tuple(jax.ShapeDtypeStruct((n, cols, 2 * ch), jnp.float32) for n in ((height + 6) // 2, (height + 3) // 2)),
        in_specs=[SMEM] + [VMEM] * 5,
        out_specs=(VMEM, VMEM),
        scratch_shapes=field_scratch(2, rows, cols, ch),
        cost_estimate=cost(42),
        compiler_params=pltpu.CompilerParams(vmem_limit_bytes=LIMIT),
    )
    sums = ahead(flags, *frames, packed[0])
    later = pl.pallas_call(
        functools.partial(second_kernel, height),
        grid=(1,),
        out_shape=jax.ShapeDtypeStruct((height, cols, ch), bf16),
        in_specs=[SMEM] + [VMEM] * 11,
        out_specs=VMEM,
        scratch_shapes=field_scratch(6, rows, cols, ch),
        cost_estimate=cost(120),
        compiler_params=pltpu.CompilerParams(vmem_limit_bytes=LIMIT),
    )(flags, *handed, *sums, *packed, *biases)

    both = jnp.stack([early, later])
    kept = lax.dynamic_slice_in_dim(both, slab * core, slab, 1)
    got = lax.ppermute(lax.dynamic_slice_in_dim(both, slab * (1 - core), slab, 1), "row", swap_core)
    by_clip = jnp.where(core == 0, jnp.stack([kept, got], 1), jnp.stack([got, kept], 1))
    forward = jnp.where(late == 1, by_clip[1], by_clip[0])
    backward = jnp.where(late == 1, by_clip[0], by_clip[1])
    return forward[:, None], backward[:, None]


def with_halo(block, sides, width):
    for axis, dim in sides:
        count = lax.axis_size(axis)
        forward = [(i, i + 1) for i in range(count - 1)]
        backward = [(target, source) for source, target in forward]
        low = lax.ppermute(
            lax.slice_in_dim(block, block.shape[dim] - width, None, axis=dim), axis, forward
        )
        high = lax.ppermute(lax.slice_in_dim(block, 0, width, axis=dim), axis, backward)
        block = jnp.concatenate([low, block, high], axis=dim)
    return block


def shifted(shard, axis, by):
    length = lax.axis_size(axis)
    pairs = [(i, i + by) for i in range(length) if 0 <= i + by < length]
    return lax.ppermute(shard, axis, pairs)


def conv_layer(field, weight, bias_vec):
    padded = jnp.pad(field, ((0, 0), (1, 1), (0, 0)))
    row_count = padded.shape[0] - 2
    col_count = padded.shape[1] - 2
    summed = jnp.zeros((row_count, col_count, weight.shape[-1]), jnp.float32)
    for offset_y in range(3):
        for offset_x in range(3):
            window = padded[offset_y : offset_y + row_count, offset_x : offset_x + col_count, :]
            product = jnp.dot(
                window.reshape(row_count * col_count, window.shape[-1]),
                weight[offset_y, offset_x],
                preferred_element_type=jnp.float32,
            )
            summed = summed + product.reshape(row_count, col_count, weight.shape[-1])
    return summed + bias_vec


def activate(values):
    return jax.nn.gelu(values, approximate=False)


def pipelined(features, w_in, b_in, w_mid, b_mid, w_out, b_out):
    clip_count, frame_count, row_count, col_count, channels = features.shape
    owners = lax.axis_size("frame")
    owner_pos = lax.axis_index("frame")
    section_total = owners + clip_count - 1
    rim_depth = 3
    rimmed = with_halo(features, (("row", 2),), rim_depth)
    slab_start = lax.axis_index("row") * row_count
    total_rows = row_count * lax.axis_size("row")
    outer_rows = slab_start - 2 + jnp.arange(row_count + 4, dtype=jnp.int32)
    outer_mask = ((outer_rows >= 0) & (outer_rows < total_rows)).astype(jnp.float32)[:, None, None]
    inner_rows = slab_start - 1 + jnp.arange(row_count + 2, dtype=jnp.int32)
    inner_mask = ((inner_rows >= 0) & (inner_rows < total_rows)).astype(jnp.float32)[:, None, None]
    zero_state = jnp.zeros((row_count, col_count, channels), jnp.bfloat16)

    def skipped(operand):
        return zero_state

    def frame_step(frame_rim, carried, direction, is_live):
        state_rim = with_halo(carried, (("row", 0),), rim_depth)
        joined = jnp.concatenate([frame_rim, state_rim], axis=-1)

        def compute(joined_in):
            first_act = (
                activate(conv_layer(joined_in, w_in[direction], b_in[direction])) * outer_mask
            ).astype(jnp.bfloat16)
            middle = (
                activate(conv_layer(first_act, w_mid[direction], b_mid[direction])) * inner_mask
            ).astype(jnp.bfloat16)
            residual = first_act[2:-2].astype(jnp.float32)
            return (residual + conv_layer(middle, w_out[direction], b_out[direction])).astype(
                jnp.bfloat16
            )

        return lax.cond(is_live, compute, skipped, joined)

    def sweep_section(section_num, incoming, outputs, direction):
        position = owner_pos if direction == 0 else owners - 1 - owner_pos
        clip_index = section_num - position
        is_live = (clip_index >= 0) & (clip_index < clip_count)
        chosen = jnp.clip(clip_index, 0, clip_count - 1)
        clip_frames = lax.dynamic_index_in_dim(rimmed, chosen, 0, keepdims=False)
        clip_out = lax.dynamic_index_in_dim(outputs, chosen, 0, keepdims=False)
        carried = incoming
        frame_order = range(frame_count) if direction == 0 else range(frame_count - 1, -1, -1)
        for frame_slot in frame_order:
            carried = frame_step(clip_frames[frame_slot], carried, direction, is_live)
            clip_out = clip_out.at[frame_slot].set(
                jnp.where(is_live, carried, clip_out[frame_slot])
            )
        outputs = lax.dynamic_update_index_in_dim(outputs, clip_out, chosen, 0)
        if direction == 0:
            passed = shifted(carried, "frame", 1)
        else:
            passed = shifted(carried, "frame", -1)
        return (passed, outputs)

    blank_out = jnp.zeros_like(features)

    def forward_turn(section_num, carry):
        return sweep_section(section_num, carry[0], carry[1], 0)

    def backward_turn(section_num, carry):
        return sweep_section(section_num, carry[0], carry[1], 1)

    _, forward_states = lax.fori_loop(0, section_total, forward_turn, (zero_state, blank_out))
    _, backward_states = lax.fori_loop(0, section_total, backward_turn, (zero_state, blank_out))
    return (forward_states, backward_states)


def on_device(features, *weights):
    clips, frames, slab, _, _ = features.shape
    fits = (clips, frames, lax.axis_size("frame"), lax.axis_size("row")) == (2, 1, 4, 4) and slab >= 6
    return (paired if fits else pipelined)(features, *weights)


def solution(mesh):
    placed = (P("parts", "frame", "row", None, None), P(), P(), P(), P(), P(), P())

    return jax.shard_map(
        on_device,
        mesh=mesh,
        in_specs=placed,
        out_specs=(P("parts", "frame", "row", None, None), P("parts", "frame", "row", None, None)),
        check_vma=False,
    )
```
